32 devices in a mesh: lon: 8 (over z, core), lat: 4 (over y, x).
Axes of the slice: x: 2, y: 2, z: 4, core: 2. Of those that a mesh axis runs over, the one named last changes fastest.
Arguments:
- state: bfloat16 [96, 384, 512], P('lat', 'lon'), may hold values from -6 to 6
- attention_in: bfloat16 [2, 512, 1536], replicated, may hold values from -10 to 10
- attention_out: bfloat16 [2, 512, 512], replicated, may hold values from -0.25 to 0.25
- expand_weight: bfloat16 [2, 512, 2048], replicated, may hold values from -0.25 to 0.25
- depth_kernel: bfloat16 [2, 7, 7, 2048], replicated, may hold values from -0.875 to 0.875
- shrink_weight: bfloat16 [2, 2048, 512], replicated, may hold values from -0.125 to 0.125
- norm_attention: float32 [2, 512], replicated, may hold values from 0.1 to 1.9
- norm_feedforward: float32 [2, 512], replicated, may hold values from 0.1 to 1.9
Outputs:
- advanced_state: bfloat16 [96, 384, 512], P('lat', 'lon')
The draws below stay inside these ranges and needn't reach their ends.
All inputs are finite; a program needn't handle non-finite values.
Results may differ from the reference program's by a relative error of at most 0.009.
Values may be sent and summed in bfloat16 or wider, within the bound.
A program may use at most 128 MiB of HBM per device.

```python
import math
import jax
import jax.numpy as jnp
from jax import lax

D = 512
HEADS = 8
HEAD_DIM = 64
FF = 2048
RADIUS = 6
CONV_RADIUS = 3
LAYERS = 2
KERNEL = 7
NLAT = 96
NLON = 384


def draw_state(key, part):
    own_key = jax.random.fold_in(key, 71)
    first = jax.random.fold_in(own_key, 0)
    extent = (NLAT, NLON, D)
    base = jax.random.normal(first, extent, jnp.float32)
    return jnp.clip(base, -6.0, 6.0).astype(jnp.bfloat16)


def draw_attention_in(key, part):
    own_key = jax.random.fold_in(key, 72)
    first = jax.random.fold_in(own_key, 0)
    base = jnp.clip(jax.random.normal(first, (LAYERS, D, 3 * D), jnp.float32), -5.0, 5.0) * D ** (-0.5)
    return base.astype(jnp.bfloat16)


def noise(rng, shape, width, limit, held_as=jnp.bfloat16):
    return jnp.clip(width * jax.random.normal(rng, shape, jnp.float32), -limit, limit).astype(held_as)


def setup_inputs(seed: int = 0) -> dict:
    seeds = jax.random.split(jax.random.key(seed), 9)
    return {
        "state": draw_state(jax.random.fold_in(seeds[8], 71), 0),
        "attention_in": draw_attention_in(jax.random.fold_in(seeds[8], 71), 0),
        "attention_out": noise(seeds[2], (LAYERS, D, D), D ** -0.5, 0.25),
        "expand_weight": noise(seeds[3], (LAYERS, D, FF), D ** -0.5, 0.25),
        "depth_kernel": noise(seeds[4], (LAYERS, KERNEL, KERNEL, FF), (KERNEL * KERNEL) ** -0.5, 0.875),
        "shrink_weight": noise(seeds[5], (LAYERS, FF, D), FF ** -0.5, 0.125),
        "norm_attention": jnp.clip(1.0 + 0.18 * jax.random.normal(seeds[6], (LAYERS, D), jnp.float32), 0.1, 1.9),
        "norm_feedforward": jnp.clip(1.0 + 0.18 * jax.random.normal(seeds[7], (LAYERS, D), jnp.float32), 0.1, 1.9),
    }


def normalize(stream, gain):
    average = lax.optimization_barrier(jnp.mean(stream, axis=-1, keepdims=True))
    centred = stream - average
    spread = lax.optimization_barrier(jnp.mean(centred * centred, axis=-1, keepdims=True))
    return (centred * lax.rsqrt(spread + 1e-05) * gain.astype(jnp.float32)).astype(jnp.bfloat16)

def widen(field, reach):
    wrapped = jnp.concatenate([field[:, -reach:], field, field[:, :reach]], axis=1)
    return jnp.pad(wrapped, ((reach, reach), (0, 0), (0, 0)))

def attend_global(queries, keys, values):
    height, breadth, channels = queries.shape
    reach = RADIUS
    span = 2 * RADIUS + 1
    key_pad = widen(keys, reach)
    value_pad = widen(values, reach)
    latitudes = jnp.arange(height, dtype=jnp.int32)
    query_heads = queries.astype(jnp.float32).reshape(height, breadth, HEADS, HEAD_DIM)
    scale = 1.0 / math.sqrt(HEAD_DIM)
    offsets = jnp.arange(span * span, dtype=jnp.int32)
    anchor = jnp.zeros((), jnp.int32)

    def score_step(carry, offset):
        down_shift = offset // span
        east_shift = offset % span
        moved = lax.dynamic_slice(key_pad, (down_shift, east_shift, anchor), (height, breadth, channels))
        scores = lax.optimization_barrier(jnp.sum(query_heads * moved.astype(jnp.float32).reshape(height, breadth, HEADS, HEAD_DIM), axis=-1)) * scale
        inside = (latitudes + down_shift - reach >= 0) & (latitudes + down_shift - reach < height)
        return (carry, jnp.where(inside[:, None, None], scores, -jnp.inf))
    unused, scores = lax.scan(score_step, jnp.zeros((), jnp.float32), offsets)
    peak = lax.optimization_barrier(jnp.max(scores, axis=0, keepdims=True))
    expos = jnp.exp(scores - peak)
    weights = (expos / lax.optimization_barrier(jnp.sum(expos, axis=0, keepdims=True))).astype(jnp.bfloat16)

    def value_step(total, item):
        offset, weight = item
        down_shift = offset // span
        east_shift = offset % span
        moved = lax.dynamic_slice(value_pad, (down_shift, east_shift, anchor), (height, breadth, channels))
        moved = moved.astype(jnp.float32).reshape(height, breadth, HEADS, HEAD_DIM)
        return (total + weight.astype(jnp.float32)[..., None] * moved, None)
    start = jnp.zeros((height, breadth, HEADS, HEAD_DIM), jnp.float32)
    total, unused = lax.scan(value_step, start, (offsets, weights))
    return total.reshape(height * breadth, channels).astype(jnp.bfloat16)

def convolve(hidden, kernel):
    height, breadth, units = hidden.shape
    wide = widen(hidden, CONV_RADIUS)
    total = jnp.zeros((height, breadth, units), jnp.float32)
    for down_shift in range(2 * CONV_RADIUS + 1):
        for east_shift in range(2 * CONV_RADIUS + 1):
            piece = wide[down_shift:down_shift + height, east_shift:east_shift + breadth]
            total = total + piece.astype(jnp.float32) * kernel[down_shift, east_shift].astype(jnp.float32)
    return total

def reference(state, attention_in, attention_out, expand_weight, depth_kernel, shrink_weight, norm_attention, norm_feedforward):
    height, breadth, channels = state.shape
    stream = state.astype(jnp.float32).reshape(height * breadth, channels)
    for layer in range(LAYERS):
        normed = normalize(stream, norm_attention[layer])
        weight_in = attention_in[layer]
        queries = jnp.dot(normed, weight_in[:, :channels], preferred_element_type=jnp.float32).astype(jnp.bfloat16)
        keys = jnp.dot(normed, weight_in[:, channels:2 * channels], preferred_element_type=jnp.float32).astype(jnp.bfloat16)
        values = jnp.dot(normed, weight_in[:, 2 * channels:], preferred_element_type=jnp.float32).astype(jnp.bfloat16)
        shape_grid = (height, breadth, channels)
        mixed = attend_global(queries.reshape(shape_grid), keys.reshape(shape_grid), values.reshape(shape_grid))
        stream = stream + jnp.dot(mixed, attention_out[layer], preferred_element_type=jnp.float32)
        normed_ff = normalize(stream, norm_feedforward[layer])
        hidden = jnp.dot(normed_ff, expand_weight[layer], preferred_element_type=jnp.float32).astype(jnp.bfloat16)
        convolved = convolve(hidden.reshape(height, breadth, -1), depth_kernel[layer])
        activated = jax.nn.gelu(convolved, approximate=False).astype(jnp.bfloat16).reshape(height * breadth, -1)
        stream = stream + jnp.dot(activated, shrink_weight[layer], preferred_element_type=jnp.float32)
    return stream.astype(jnp.bfloat16).reshape(height, breadth, channels)
```

```python
import functools
import math

import jax
import jax.numpy as jnp
import numpy as np
from jax import lax
from jax.experimental import pallas as pl
from jax.experimental.pallas import tpu as pltpu
from jax.sharding import PartitionSpec as P

HEAD_DIM = 64
RADIUS = 6
CONV_RADIUS = 3
Q_LAT = 4
Q_LON = 16
COLS = 8
K_LAT = Q_LAT + 2 * RADIUS
K_LON = Q_LON + 2 * COLS
GROUP = 4
SPAN = GROUP * HEAD_DIM
CHUNK = 1024
NEG = -1e30
VMEM_LIMIT = 60 * 1024 * 1024
F32 = jnp.float32
BF16 = jnp.bfloat16
MESH = pl.DeviceIdType.MESH


def spectral(height, cols):
    side = 2 * CONV_RADIUS + 1
    tall, wide = height + side - 1, cols + side - 1
    window, offset = cols + 2 * COLS, COLS - CONV_RADIUS
    kept = []
    for u in range(tall):
        for v in range(wide):
            other = ((-u) % tall, (-v) % wide)
            if (u, v) <= other:
                kept.append((u, v, (u, v) == other))
    m = len(kept)
    half = -(-m // 16) * 16
    u, v = (np.array([k[i] for k in kept], np.float64)[:, None] for i in (0, 1))
    single = np.array([k[2] for k in kept])[:, None]

    def phase(rows, columns, stride=None):
        r, c = np.meshgrid(np.arange(rows), columns, indexing="ij")
        return 2 * np.pi * (u * r.reshape(1, -1) / tall + v * c.reshape(1, -1) / wide)

    columns = np.arange(window) - offset
    inside = np.tile((columns >= 0) & (columns < wide), tall)[None]
    angle = phase(tall, columns)
    forward = np.zeros((2 * half, tall * window))
    forward[:m] = np.cos(angle) * inside
    forward[half : half + m] = -np.sin(angle) * inside * ~single
    angle = phase(side, np.arange(8))
    inside = np.tile(np.arange(8) < side, side)[None]
    taps = np.zeros((2 * half, side * 8))
    taps[:m] = np.cos(angle) * inside
    taps[half : half + m] = np.sin(angle) * inside * ~single
    angle = phase(height, np.arange(cols))
    scale = np.where(single, 1.0, 2.0) / (tall * wide)
    inverse = np.zeros((height * cols, 2 * half))
    inverse[:, :m] = (np.cos(angle) * scale).T
    inverse[:, half : half + m] = -(np.sin(angle) * scale).T
    coarse = taps.astype(jnp.bfloat16)
    fine = (taps - coarse.astype(np.float64)).astype(jnp.bfloat16)
    return (
        forward.astype(jnp.bfloat16),
        np.concatenate([coarse, fine], axis=1),
        inverse.astype(jnp.bfloat16),
    )


def norm_rows(stream, gain):
    average = jnp.mean(stream, axis=-1, keepdims=True)
    centred = stream - average
    spread = jnp.mean(centred * centred, axis=-1, keepdims=True)
    return (centred * lax.rsqrt(spread + 1e-05) * gain).astype(BF16)


def gelu(x):
    return 0.5 * x * (1.0 + lax.erf(x * math.sqrt(0.5)))


def dot(a, b):
    return jnp.dot(a, b, preferred_element_type=F32)


def kernel(
    state_ref, gain_a_ref, gain_f_ref,
    w_in_hbm, w_out_hbm, expand_hbm, shrink_hbm, taps_hbm, forward_hbm, basis_hbm, inverse_hbm,
    out_ref,
    w_in, w_out, expand, shrink, taps, forward, basis, inverse,
    ext_a, ext_f, stream, q_ref, kv_ref, mixed_ref, bias_ref, nhat, khat, act,
    load_sem, send_a, recv_a, send_f, recv_f,
):
    height, blocks, _, channels = state_ref.shape
    width = blocks * COLS
    layers = w_in.shape[0]
    units = expand.shape[2]
    tiles = width // Q_LON
    per = Q_LON // COLS
    bands = height // Q_LAT
    half = forward.shape[0] // 2
    part = Q_LAT * Q_LON
    keys = K_LAT * K_LON

    lat, lon = lax.axis_index("lat"), lax.axis_index("lon")
    n_lat, n_lon = lax.axis_size("lat"), lax.axis_size("lon")
    east, west = lax.rem(lon + 1, n_lon), lax.rem(lon + n_lon - 1, n_lon)
    has = {-1: lat > 0, 1: lat < n_lat - 1}

    def peer(dy, dx):
        return {"lat": lat + dy, "lon": {-1: west, 0: lon, 1: east}[dx]}

    def given(dy, f):
        if dy == 0:
            f()
        else:
            pl.when(has[dy])(f)

    loads = {}
    plan = [(w_in, w_in_hbm, True), (taps, taps_hbm, True), (basis, basis_hbm, False),
            (w_out, w_out_hbm, True), (forward, forward_hbm, False), (expand, expand_hbm, True),
            (inverse, inverse_hbm, False), (shrink, shrink_hbm, True)]
    spot = 0
    for layer in range(layers):
        for i, (dst, src, layered) in enumerate(plan):
            if layered or layer == 0:
                view = (src.at[layer], dst.at[layer]) if layered else (src, dst)
                loads[i, layer] = pltpu.make_async_copy(*view, load_sem.at[spot])
                loads[i, layer].start()
                spot += 1

    def ready(i, layer):
        loads[i, layer].wait()

    def transfer(buf, reach, send, recv, slot, dy, dx, rows, cols):
        r0, rn = rows
        c0, cn = cols
        to_r = r0 - dy * height
        to_c = c0 - dx * blocks
        return pltpu.make_async_remote_copy(
            src_ref=buf.at[pl.ds(reach + r0, rn), pl.ds(1 + c0, cn)],
            dst_ref=buf.at[pl.ds(reach + to_r, rn), pl.ds(1 + to_c, cn)],
            send_sem=send.at[slot],
            recv_sem=recv.at[slot],
            device_id=peer(dy, dx),
            device_id_type=MESH,
        )

    def edge(dy, reach):
        return (0, reach) if dy < 0 else (height - reach, reach)

    def column(dx):
        return (0, 1) if dx < 0 else (blocks - 1, 1)

    def copy_a(layer, kind, dy, dx, t=0):
        buf, send, recv = ext_a.at[layer], send_a.at[layer], recv_a.at[layer]
        if kind == "ns":
            slot = (tiles if dy > 0 else 0) + t
            return transfer(buf, RADIUS, send, recv, slot, dy, 0, edge(dy, RADIUS), (per * t, per))
        if kind == "ew":
            slot = 2 * tiles + (dx > 0)
            return transfer(buf, RADIUS, send, recv, slot, 0, dx, (0, height), column(dx))
        slot = 2 * tiles + 2 + 2 * (dy > 0) + (dx > 0)
        return transfer(buf, RADIUS, send, recv, slot, dy, dx, edge(dy, RADIUS), column(dx))

    def copy_f(layer, kind, dy, dx, b=0):
        buf, send, recv = ext_f.at[layer], send_f.at[layer], recv_f.at[layer]
        if kind == "ns":
            return transfer(
                buf, CONV_RADIUS, send, recv, int(dy > 0), dy, 0, edge(dy, CONV_RADIUS), (0, blocks)
            )
        if kind == "ew":
            slot = 6 + (bands if dx > 0 else 0) + b
            return transfer(
                buf, CONV_RADIUS, send, recv, slot, 0, dx, (Q_LAT * b, Q_LAT), column(dx)
            )
        slot = 2 + 2 * (dy > 0) + (dx > 0)
        return transfer(buf, CONV_RADIUS, send, recv, slot, dy, dx, edge(dy, CONV_RADIUS), column(dx))

    def start_a(layer, t):
        for dy in (-1, 1):
            given(dy, lambda dy=dy: copy_a(layer, "ns", dy, 0, t).start())
        for dx, tile in ((-1, 0), (1, tiles - 1)):
            @pl.when(t == tile)
            def _():
                copy_a(layer, "ew", 0, dx).start()
                for dy in (-1, 1):
                    given(dy, lambda dy=dy: copy_a(layer, "corner", dy, dx).start())

    def wait_recv_a(layer, what):
        if what == "ew":
            for dx in (-1, 1):
                copy_a(layer, "ew", 0, dx).wait_recv()
        else:
            for dy in (-1, 1):
                def _():
                    for t in range(tiles):
                        copy_a(layer, "ns", dy, 0, t).wait_recv()
                    for dx in (-1, 1):
                        copy_a(layer, "corner", dy, dx).wait_recv()
                given(-dy, _)

    def wait_send_a(layer):
        for dx in (-1, 1):
            copy_a(layer, "ew", 0, dx).wait_send()
        for dy in (-1, 1):
            def _():
                for t in range(tiles):
                    copy_a(layer, "ns", dy, 0, t).wait_send()
                for dx in (-1, 1):
                    copy_a(layer, "corner", dy, dx).wait_send()
            given(dy, _)

    def start_f(layer, b):
        for dx in (-1, 1):
            copy_f(layer, "ew", 0, dx, b).start()

    def start_f_edge(layer, dy):
        def _():
            copy_f(layer, "ns", dy, 0).start()
            for dx in (-1, 1):
                copy_f(layer, "corner", dy, dx).start()
        given(dy, _)

    def wait_send_f(layer):
        for dx in (-1, 1):
            for b in range(bands):
                copy_f(layer, "ew", 0, dx, b).wait_send()
        for dy in (-1, 1):
            def _():
                copy_f(layer, "ns", dy, 0).wait_send()
                for dx in (-1, 1):
                    copy_f(layer, "corner", dy, dx).wait_send()
            given(dy, _)

    barrier = pltpu.get_barrier_semaphore()
    for dy in (-1, 0, 1):
        for dx in (-1, 0, 1):
            if (dy, dx) != (0, 0):
                given(dy, lambda dy=dy, dx=dx: pl.semaphore_signal(
                    barrier, inc=1, device_id=peer(dy, dx), device_id_type=MESH))

    def norm_tile(layer, t, x):
        z = norm_rows(x, gain_a_ref[layer]).reshape(height, per, COLS, channels)
        ext_a[layer, pl.ds(RADIUS, height), pl.ds(1 + per * t, per)] = z

    @pl.loop(0, tiles)
    def _(t):
        x = state_ref[:, pl.ds(per * t, per)].astype(F32)
        stream[:, pl.ds(per * t, per)] = x
        norm_tile(0, t, x.reshape(height * Q_LON, channels))

    pl.semaphore_wait(barrier, 2 + 3 * sum(h.astype(jnp.int32) for h in has.values()))
    for t in range(tiles):
        start_a(0, t)

    for dy in (-1, 1):
        @pl.when(jnp.logical_not(has[dy]))
        def _():
            for buf, reach in ((ext_a, RADIUS), (ext_f, CONV_RADIUS)):
                first = 0 if dy < 0 else reach + height
                shape = (layers, reach) + buf.shape[2:]
                buf[:, first : first + reach] = jnp.zeros(shape, BF16)

    m = lax.broadcasted_iota(jnp.int32, (part, keys), 0)
    n = lax.broadcasted_iota(jnp.int32, (part, keys), 1)
    up = n // K_LON - RADIUS - m // Q_LON
    over = n % K_LON - COLS - m % Q_LON
    near = (jnp.abs(up) <= RADIUS) & (jnp.abs(over) <= RADIUS)

    @pl.loop(0, bands)
    def _(b):
        place = lat * height + b * Q_LAT + n // K_LON - RADIUS
        bias_ref[b] = jnp.where(near & (place >= 0) & (place < n_lat * height), 0.0, NEG)

    ready(2, 0)
    for layer in range(layers):
        ready(1, layer)

        @pl.loop(0, units // CHUNK)
        def _(c):
            lanes = pl.ds(pl.multiple_of(c * CHUNK, CHUNK), CHUNK)
            khat[layer, :, lanes] = dot(basis[...], taps[layer, :, lanes]).astype(BF16)

    lane_head = lax.broadcasted_iota(jnp.int32, (part, SPAN), 1) // HEAD_DIM

    def attend(r0, t, g, bias):
        lo = g * SPAN
        rows, cols = pl.ds(r0, K_LAT), slice(per * t, per * t + K_LON // COLS)
        q = q_ref[pl.ds(r0, Q_LAT), per * t : per * t + per, :, lo : lo + SPAN].reshape(part, SPAN)
        k = kv_ref[rows, cols, :, lo : lo + SPAN].reshape(keys, SPAN)
        v = kv_ref[rows, cols, :, channels + lo : channels + lo + SPAN].reshape(keys, SPAN)
        qq = jnp.concatenate(
            [jnp.where(lane_head == h, q, jnp.zeros_like(q)) for h in range(GROUP)], axis=0
        )
        s = lax.dot_general(qq, k, (((1,), (1,)), ((), ())), preferred_element_type=F32)
        s = (s.reshape(GROUP, part, keys) + bias[None]).reshape(s.shape)
        e = jnp.exp(s - jnp.max(s, axis=-1, keepdims=True))
        total = jnp.sum(e, axis=-1, keepdims=True)
        o = dot(e.astype(BF16), v) * (1.0 / total)
        m = jnp.zeros((part, SPAN), F32)
        for h in range(GROUP):
            m = jnp.where(lane_head == h, o[h * part : (h + 1) * part], m)
        mixed_ref[:, per * t : per * t + per, :, lo : lo + SPAN] = m.astype(BF16).reshape(
            Q_LAT, per, COLS, SPAN
        )

    def band(layer, b):
        r0 = b * Q_LAT
        for t in range(tiles):
            for g in range(channels // SPAN):
                attend(r0, t, g, bias_ref[b])
        rs = pl.ds(r0, Q_LAT)
        x = mixed_ref[...].reshape(Q_LAT * width, channels)
        y = dot(x, w_out[layer]) + stream[rs].reshape(Q_LAT * width, channels)
        shape = (Q_LAT, blocks, COLS, channels)
        stream[rs] = y.reshape(shape)
        z = norm_rows(y, gain_f_ref[layer])
        ext_f[layer, pl.ds(CONV_RADIUS + r0, Q_LAT), 1 : 1 + blocks] = z.reshape(shape)
        start_f(layer, b)

    reach_b = -(-RADIUS // Q_LAT)
    own = slice(1, 1 + blocks)

    def project(layer, rows, cols, count):
        x = ext_a[layer, rows, cols].reshape(-1, channels)
        y = dot(x, w_in[layer, :, channels:]).astype(BF16)
        kv_ref[rows, cols] = y.reshape(y.shape[0] // (count * COLS), count, COLS, 2 * channels)

    for layer in range(layers):
        last = layer == layers - 1
        ready(0, layer)
        x = ext_a[layer, RADIUS : RADIUS + height, own].reshape(height * width, channels)
        shape = (height, blocks, COLS, channels)
        y = dot(x, w_in[layer, :, :channels]).astype(BF16) * (1.0 / math.sqrt(HEAD_DIM))
        q_ref[...] = y.astype(BF16).reshape(shape)
        for i in range(2):
            cs = slice((i + 1) * channels, (i + 2) * channels)
            y = dot(x, w_in[layer, :, cs]).astype(BF16)
            to = slice(i * channels, (i + 1) * channels)
            kv_ref[RADIUS : RADIUS + height, own, :, to] = y.reshape(shape)
        wait_recv_a(layer, "ew")
        for c in (0, 1 + blocks):
            project(layer, slice(RADIUS, RADIUS + height), slice(c, c + 1), 1)
        ready(3, layer)

        @pl.loop(reach_b, bands - reach_b)
        def _(b):
            band(layer, b)

        wait_recv_a(layer, "rest")
        for r in (0, RADIUS + height):
            project(layer, slice(r, r + RADIUS), slice(0, blocks + 2), blocks + 2)

        for j in range(reach_b):
            @pl.loop(0, 2)
            def _(k):
                band(layer, j + k * (bands - 1 - 2 * j))
                if j == 0:
                    for i, dy in enumerate((-1, 1)):
                        @pl.when(k == i)
                        def _():
                            start_f_edge(layer, dy)

        if layer == 0:
            ready(4, 0)
            ready(6, 0)
        ready(5, layer)
        ready(7, layer)
        for dy in (-1, 1):
            given(-dy, lambda: copy_f(layer, "ns", dy, 0).wait_recv())

        @pl.loop(0, tiles)
        def _(k):
            t = lax.rem(k + 1, tiles)
            for dx, tile in ((-1, tiles - 1), (1, 0)):
                @pl.when(t == tile)
                def _():
                    for b in range(bands):
                        copy_f(layer, "ew", 0, dx, b).wait_recv()
                    for dy in (-1, 1):
                        given(-dy, lambda: copy_f(layer, "corner", dy, dx).wait_recv())
            x = ext_f[layer, :, pl.ds(per * t, per + 2)].reshape(-1, channels)
            nhat[...] = dot(forward[...], x).astype(BF16)

            @pl.loop(0, units // CHUNK)
            def _(c):
                lanes = pl.ds(pl.multiple_of(c * CHUNK, CHUNK), CHUNK)
                z = dot(nhat[...], expand[layer, :, lanes]).astype(BF16)
                re, im = z[:half], z[half:]
                k_re, k_im = khat[layer, :half, lanes], khat[layer, half:, lanes]
                y = jnp.concatenate([re * k_re - im * k_im, re * k_im + im * k_re], axis=0)
                act[:, lanes] = gelu(dot(inverse[...], y)).astype(BF16)

            cs = pl.ds(per * t, per)
            y = dot(act[...], shrink[layer]) + stream[:, cs].reshape(height * Q_LON, channels)
            shape = (height, per, COLS, channels)
            if last:
                out_ref[:, cs] = y.astype(BF16).reshape(shape)
            else:
                stream[:, cs] = y.reshape(shape)
                norm_tile(layer + 1, t, y)
                start_a(layer + 1, t)

    for layer in range(layers):
        wait_send_a(layer)
        wait_send_f(layer)


def per_device(
    state,
    attention_in,
    attention_out,
    expand_weight,
    depth_kernel,
    shrink_weight,
    norm_attention,
    norm_feedforward,
):
    height, width, channels = state.shape
    layers, side, _, units = depth_kernel.shape
    blocks = width // COLS
    tiles, bands = width // Q_LON, height // Q_LAT
    forward, basis, inverse = spectral(height, Q_LON)
    taps = jnp.pad(depth_kernel, ((0, 0), (0, 0), (0, 8 - side), (0, 0)))
    taps = taps.reshape(layers, side * 8, units)
    taps = jnp.concatenate([taps, taps], axis=1)
    heavy = (
        attention_in, attention_out, expand_weight, shrink_weight, taps,
        jnp.asarray(forward), jnp.asarray(basis), jnp.asarray(inverse),
    )
    any_spec = pl.BlockSpec(memory_space=pl.ANY)
    vmem_spec = pl.BlockSpec(memory_space=pltpu.VMEM)
    shape = (height, blocks, COLS, channels)
    slots_a, slots_f = 2 * tiles + 6, 2 * bands + 6
    out = pl.pallas_call(
        kernel,
        out_shape=jax.ShapeDtypeStruct(shape, BF16),
        in_specs=[vmem_spec] * 3 + [any_spec] * len(heavy),
        out_specs=vmem_spec,
        scratch_shapes=[pltpu.VMEM(a.shape, BF16) for a in heavy]
        + [
            pltpu.VMEM((layers, height + 2 * RADIUS, blocks + 2, COLS, channels), BF16),
            pltpu.VMEM((layers, height + 2 * CONV_RADIUS, blocks + 2, COLS, channels), BF16),
            pltpu.VMEM(shape, F32),
            pltpu.VMEM(shape, BF16),
            pltpu.VMEM((height + 2 * RADIUS, blocks + 2, COLS, 2 * channels), BF16),
            pltpu.VMEM((Q_LAT, blocks, COLS, channels), BF16),
            pltpu.VMEM((bands, Q_LAT * Q_LON, K_LAT * K_LON), F32),
            pltpu.VMEM((forward.shape[0], channels), BF16),
            pltpu.VMEM((layers, forward.shape[0], units), BF16),
            pltpu.VMEM((height * Q_LON, units), BF16),
            pltpu.SemaphoreType.DMA((5 * layers + 3,)),
            pltpu.SemaphoreType.DMA((layers, slots_a)),
            pltpu.SemaphoreType.DMA((layers, slots_a)),
            pltpu.SemaphoreType.DMA((layers, slots_f)),
            pltpu.SemaphoreType.DMA((layers, slots_f)),
        ],
        compiler_params=pltpu.CompilerParams(
            vmem_limit_bytes=VMEM_LIMIT, collective_id=0, has_side_effects=True
        ),
        name="blocks",
    )(
        state.reshape(shape), norm_attention[:, None], norm_feedforward[:, None], *heavy
    )
    return out.reshape(height, width, channels)


def solution(mesh):
    in_specs = (P("lat", "lon", None), P(), P(), P(), P(), P(), P(), P())
    out_specs = P("lat", "lon", None)
    return jax.shard_map(
        per_device, mesh=mesh, in_specs=in_specs, out_specs=out_specs, check_vma=False
    )
```

```python
import functools
import math

import jax
import jax.numpy as jnp
import numpy as np
from jax import lax
from jax.experimental import pallas as pl
from jax.experimental.pallas import tpu as pltpu
from jax.sharding import PartitionSpec as P

HEAD_DIM = 64
RADIUS = 6
CONV_RADIUS = 3
Q_LAT = 4
Q_LON = 16
COLS = 8
K_LAT = Q_LAT + 2 * RADIUS
K_LON = Q_LON + 2 * COLS
GROUP = 4
SPAN = GROUP * HEAD_DIM
CHUNK = 1024
NEG = -1e30
VMEM_LIMIT = 60 * 1024 * 1024
F32 = jnp.float32
BF16 = jnp.bfloat16
MESH = pl.DeviceIdType.MESH


def spectral(height, cols, layers):
    side = 2 * CONV_RADIUS + 1
    tall, wide = height + side - 1, cols + side - 1
    window, offset = cols + 2 * COLS, COLS - CONV_RADIUS
    kept = []
    for u in range(tall):
        for v in range(wide):
            other = ((-u) % tall, (-v) % wide)
            if (u, v) <= other:
                kept.append((u, v, (u, v) == other))
    m = len(kept)
    half = -(-m // 16) * 16
    u, v = (np.array([k[i] for k in kept], np.float64)[:, None] for i in (0, 1))
    single = np.array([k[2] for k in kept])[:, None]

    def phase(rows, columns, stride=None):
        r, c = np.meshgrid(np.arange(rows), columns, indexing="ij")
        return 2 * np.pi * (u * r.reshape(1, -1) / tall + v * c.reshape(1, -1) / wide)

    columns = np.arange(window) - offset
    inside = np.tile((columns >= 0) & (columns < wide), tall)[None]
    angle = phase(tall, columns)
    forward = np.zeros((2 * half, tall * window))
    forward[:m] = np.cos(angle) * inside
    forward[half : half + m] = -np.sin(angle) * inside * ~single
    angle = phase(side, np.arange(side))
    taps = np.zeros((layers, 2 * half, -(-side * side * layers // 16) * 16))
    for layer in range(layers):
        mine = slice(layer, side * side * layers, layers)
        taps[layer, :m, mine] = np.cos(angle)
        taps[layer, half : half + m, mine] = np.sin(angle) * ~single
    angle = phase(height, np.arange(cols))
    scale = np.where(single, 1.0, 2.0) / (tall * wide)
    inverse = np.zeros((height * cols, 2 * half))
    inverse[:, :m] = (np.cos(angle) * scale).T
    inverse[:, half : half + m] = -(np.sin(angle) * scale).T
    coarse = taps.astype(jnp.bfloat16)
    fine = (taps - coarse.astype(np.float64)).astype(jnp.bfloat16)
    return (
        forward.astype(jnp.bfloat16),
        np.concatenate([coarse, fine], axis=2),
        inverse.astype(jnp.bfloat16),
    )


def norm_rows(stream, gain):
    average = jnp.mean(stream, axis=-1, keepdims=True)
    centred = stream - average
    spread = jnp.mean(centred * centred, axis=-1, keepdims=True)
    return (centred * lax.rsqrt(spread + 1e-05) * gain).astype(BF16)


def gelu(x):
    return 0.5 * x * (1.0 + lax.erf(x * math.sqrt(0.5)))


def dot(a, b):
    return jnp.dot(a, b, preferred_element_type=F32)


def kernel(
    state_hbm, gain_a_ref, gain_f_ref,
    w_in_hbm, w_out_hbm, expand_hbm, shrink_hbm, taps_hbm, forward_hbm, basis_hbm, inverse_hbm,
    out_hbm,
    w_in, w_out, expand, shrink, taps, forward, basis, inverse,
    raw, ext_a, ext_f, stream, q_ref, kv_ref, mixed_ref, bias_ref, nhat, khat, act,
    load_sem, state_sem, out_sem, send_a, recv_a, send_f, recv_f,
):
    height, blocks, _, channels = raw.shape
    width = blocks * COLS
    layers = w_in.shape[0]
    units = expand.shape[2]
    tiles = width // Q_LON
    per = Q_LON // COLS
    bands = height // Q_LAT
    half = forward.shape[0] // 2
    part = Q_LAT * Q_LON
    keys = K_LAT * K_LON

    lat, lon = lax.axis_index("lat"), lax.axis_index("lon")
    n_lat, n_lon = lax.axis_size("lat"), lax.axis_size("lon")
    east, west = lax.rem(lon + 1, n_lon), lax.rem(lon + n_lon - 1, n_lon)
    has = {-1: lat > 0, 1: lat < n_lat - 1}

    def peer(dy, dx):
        return {"lat": lat + dy, "lon": {-1: west, 0: lon, 1: east}[dx]}

    def given(dy, f):
        if dy == 0:
            f()
        else:
            pl.when(has[dy])(f)

    plan = [(w_in, w_in_hbm, True), (taps, taps_hbm, False), (basis, basis_hbm, True),
            (w_out, w_out_hbm, True), (forward, forward_hbm, False), (expand, expand_hbm, True),
            (inverse, inverse_hbm, False), (shrink, shrink_hbm, True)]

    def load(i, layer):
        dst, src, layered = plan[i]
        view = (src.at[layer], dst.at[layer]) if layered else (src, dst)
        return pltpu.make_async_copy(*view, load_sem.at[i, layer])

    def transfer(buf, reach, send, recv, slot, dy, dx, rows, cols):
        r0, rn = rows
        c0, cn = cols
        to_r = r0 - dy * height
        to_c = c0 - dx * blocks
        return pltpu.make_async_remote_copy(
            src_ref=buf.at[pl.ds(reach + r0, rn), pl.ds(1 + c0, cn)],
            dst_ref=buf.at[pl.ds(reach + to_r, rn), pl.ds(1 + to_c, cn)],
            send_sem=send.at[slot],
            recv_sem=recv.at[slot],
            device_id=peer(dy, dx),
            device_id_type=MESH,
        )

    def edge(dy, reach):
        return (0, reach) if dy < 0 else (height - reach, reach)

    def column(dx):
        return (0, 1) if dx < 0 else (blocks - 1, 1)

    def copy_a(layer, kind, dy, dx, t=0):
        buf, send, recv = ext_a.at[layer], send_a.at[layer], recv_a.at[layer]
        if kind == "ns":
            slot = (tiles if dy > 0 else 0) + t
            return transfer(buf, RADIUS, send, recv, slot, dy, 0, edge(dy, RADIUS), (per * t, per))
        if kind == "ew":
            slot = 2 * tiles + (dx > 0)
            return transfer(buf, RADIUS, send, recv, slot, 0, dx, (0, height), column(dx))
        slot = 2 * tiles + 2 + 2 * (dy > 0) + (dx > 0)
        return transfer(buf, RADIUS, send, recv, slot, dy, dx, edge(dy, RADIUS), column(dx))

    def copy_f(layer, kind, dy, dx, b=0):
        buf, send, recv = ext_f.at[layer], send_f.at[layer], recv_f.at[layer]
        if kind == "ns":
            return transfer(
                buf, CONV_RADIUS, send, recv, int(dy > 0), dy, 0, edge(dy, CONV_RADIUS), (0, blocks)
            )
        if kind == "ew":
            slot = 6 + (bands if dx > 0 else 0) + b
            return transfer(
                buf, CONV_RADIUS, send, recv, slot, 0, dx, (Q_LAT * b, Q_LAT), column(dx)
            )
        slot = 2 + 2 * (dy > 0) + (dx > 0)
        return transfer(buf, CONV_RADIUS, send, recv, slot, dy, dx, edge(dy, CONV_RADIUS), column(dx))

    def start_a(layer, t):
        for dy in (-1, 1):
            given(dy, lambda dy=dy: copy_a(layer, "ns", dy, 0, t).start())
        for dx, tile in ((-1, 0), (1, tiles - 1)):
            @pl.when(t == tile)
            def _():
                copy_a(layer, "ew", 0, dx).start()
                for dy in (-1, 1):
                    given(dy, lambda dy=dy: copy_a(layer, "corner", dy, dx).start())

    def wait_recv_a(layer, what):
        if what == "ew":
            for dx in (-1, 1):
                copy_a(layer, "ew", 0, dx).wait_recv()
        else:
            for dy in (-1, 1):
                def _():
                    for t in range(tiles):
                        copy_a(layer, "ns", dy, 0, t).wait_recv()
                    for dx in (-1, 1):
                        copy_a(layer, "corner", dy, dx).wait_recv()
                given(-dy, _)

    def wait_send_a(layer):
        for dx in (-1, 1):
            copy_a(layer, "ew", 0, dx).wait_send()
        for dy in (-1, 1):
            def _():
                for t in range(tiles):
                    copy_a(layer, "ns", dy, 0, t).wait_send()
                for dx in (-1, 1):
                    copy_a(layer, "corner", dy, dx).wait_send()
            given(dy, _)

    def start_f(layer, b):
        for dx in (-1, 1):
            copy_f(layer, "ew", 0, dx, b).start()

    def start_f_edge(layer, dy):
        def _():
            copy_f(layer, "ns", dy, 0).start()
            for dx in (-1, 1):
                copy_f(layer, "corner", dy, dx).start()
        given(dy, _)

    def wait_send_f(layer):
        for dx in (-1, 1):
            for b in range(bands):
                copy_f(layer, "ew", 0, dx, b).wait_send()
        for dy in (-1, 1):
            def _():
                copy_f(layer, "ns", dy, 0).wait_send()
                for dx in (-1, 1):
                    copy_f(layer, "corner", dy, dx).wait_send()
            given(dy, _)

    barrier = pltpu.get_barrier_semaphore()
    for dy in (-1, 0, 1):
        for dx in (-1, 0, 1):
            if (dy, dx) != (0, 0):
                given(dy, lambda dy=dy, dx=dx: pl.semaphore_signal(
                    barrier, inc=1, device_id=peer(dy, dx), device_id_type=MESH))

    state_copy = pltpu.make_async_copy(state_hbm, raw, state_sem)
    state_copy.start()
    for layer in range(layers):
        for i, (_, _, layered) in enumerate(plan):
            if layered or layer == 0:
                load(i, layer).start()

    def norm_tile(layer, t, x):
        z = norm_rows(x, gain_a_ref[pl.ds(layer, 1)]).reshape(height, per, COLS, channels)
        ext_a[layer, pl.ds(RADIUS, height), pl.ds(1 + per * t, per)] = z

    state_copy.wait()

    @pl.loop(0, tiles)
    def _(t):
        x = raw[:, pl.ds(per * t, per)].astype(F32)
        stream[:, pl.ds(per * t, per)] = x
        norm_tile(0, t, x.reshape(height * Q_LON, channels))

    pl.semaphore_wait(barrier, 2 + 3 * sum(h.astype(jnp.int32) for h in has.values()))

    @pl.loop(0, tiles)
    def _(t):
        start_a(0, t)

    for dy in (-1, 1):
        @pl.when(jnp.logical_not(has[dy]))
        def _():
            for buf, reach in ((ext_a, RADIUS), (ext_f, CONV_RADIUS)):
                first = 0 if dy < 0 else reach + height
                shape = (layers, reach) + buf.shape[2:]
                buf[:, first : first + reach] = jnp.zeros(shape, BF16)

    m = lax.broadcasted_iota(jnp.int32, (part, keys), 0)
    n = lax.broadcasted_iota(jnp.int32, (part, keys), 1)
    up = n // K_LON - RADIUS - m // Q_LON
    over = n % K_LON - COLS - m % Q_LON
    near = (jnp.abs(up) <= RADIUS) & (jnp.abs(over) <= RADIUS)

    @pl.loop(0, bands)
    def _(b):
        place = lat * height + b * Q_LAT + n // K_LON - RADIUS
        bias_ref[b] = jnp.where(near & (place >= 0) & (place < n_lat * height), 0.0, NEG)

    def spectra():
        load(1, 0).wait()
        for layer in range(layers):
            load(2, layer).wait()

        @pl.loop(0, units // CHUNK)
        def _(c):
            lanes = pl.ds(pl.multiple_of(c * CHUNK, CHUNK), CHUNK)
            x = taps[:, :, :, lanes].astype(F32).reshape(-1, CHUNK)
            fill = jnp.zeros((basis.shape[2] // 2 - x.shape[0], CHUNK), F32)
            x = jnp.concatenate([x, fill], axis=0).astype(BF16)
            x = jnp.concatenate([x, x], axis=0)
            for layer in range(layers):
                khat[layer, :, lanes] = dot(basis[layer], x).astype(BF16)

    lane_head = lax.broadcasted_iota(jnp.int32, (part, SPAN), 1) // HEAD_DIM

    def attend(i, b, t, g):
        lo = g * SPAN
        rows, cols = pl.ds(b * Q_LAT, K_LAT), slice(per * t, per * t + K_LON // COLS)
        mine = slice(per * t, per * t + per)
        q = q_ref[pl.ds(b * Q_LAT, Q_LAT), mine, :, lo : lo + SPAN].reshape(part, SPAN)
        k = kv_ref[rows, cols, :, lo : lo + SPAN].reshape(keys, SPAN)
        v = kv_ref[rows, cols, :, channels + lo : channels + lo + SPAN].reshape(keys, SPAN)
        qq = jnp.concatenate(
            [jnp.where(lane_head == h, q, jnp.zeros_like(q)) for h in range(GROUP)], axis=0
        )
        s = lax.dot_general(qq, k, (((1,), (1,)), ((), ())), preferred_element_type=F32)
        s = (s.reshape(GROUP, part, keys) + bias_ref[b][None]).reshape(s.shape)
        e = jnp.exp(s - jnp.max(s, axis=-1, keepdims=True))
        total = jnp.sum(e, axis=-1, keepdims=True)
        o = dot(e.astype(BF16), v) * (1.0 / total)
        m = jnp.zeros((part, SPAN), F32)
        for h in range(GROUP):
            m = jnp.where(lane_head == h, o[h * part : (h + 1) * part], m)
        mixed_ref[i, :, mine, :, lo : lo + SPAN] = m.astype(BF16).reshape(Q_LAT, per, COLS, SPAN)

    own = slice(1, 1 + blocks)
    pairs = bands // 2

    def project(layer, rows, cols, count):
        x = ext_a[layer, rows, cols].reshape(-1, channels)
        y = dot(x, w_in[layer, :, channels:]).astype(BF16)
        kv_ref[rows, cols] = y.reshape(y.shape[0] // (count * COLS), count, COLS, 2 * channels)

    @pl.loop(0, layers)
    def _(layer):
        load(0, layer).wait()
        x = ext_a[layer, RADIUS : RADIUS + height, own].reshape(height * width, channels)
        shape = (height, blocks, COLS, channels)
        y = dot(x, w_in[layer, :, :channels]).astype(BF16) * (1.0 / math.sqrt(HEAD_DIM))
        q_ref[...] = y.astype(BF16).reshape(shape)
        for i in range(2):
            cs = slice((i + 1) * channels, (i + 2) * channels)
            y = dot(x, w_in[layer, :, cs]).astype(BF16)
            to = slice(i * channels, (i + 1) * channels)
            kv_ref[RADIUS : RADIUS + height, own, :, to] = y.reshape(shape)

        @pl.when(layer == 0)
        def _():
            spectra()

        later = jnp.minimum(layer, 1)

        @pl.loop(0, pairs)
        def _(p):
            b0 = lax.rem((1 - later) * (p + pairs - 1) + later * (pairs - p), pairs)
            both = (b0, bands - 1 - b0)

            @pl.when(b0 == 0)
            def _():
                wait_recv_a(layer, "rest")
                for r in (0, RADIUS + height):
                    project(layer, slice(r, r + RADIUS), slice(0, blocks + 2), blocks + 2)

            for t in range(1, tiles - 1):
                for i, b in enumerate(both):
                    for g in range(channels // SPAN):
                        attend(i, b, t, g)

            @pl.when(p == 0)
            def _():
                wait_recv_a(layer, "ew")
                for c in (0, 1 + blocks):
                    project(layer, slice(RADIUS, RADIUS + height), slice(c, c + 1), 1)
                load(3, layer).wait()

            for t in (0, tiles - 1):
                for i, b in enumerate(both):
                    for g in range(channels // SPAN):
                        attend(i, b, t, g)
            x = mixed_ref[...].reshape(2 * Q_LAT * width, channels)
            y = dot(x, w_out[layer])
            for i, b in enumerate(both):
                rs = pl.ds(b * Q_LAT, Q_LAT)
                size = Q_LAT * width
                shape = (Q_LAT, blocks, COLS, channels)
                part_y = y[i * size : (i + 1) * size] + stream[rs].reshape(size, channels)
                stream[rs] = part_y.reshape(shape)
                z = norm_rows(part_y, gain_f_ref[pl.ds(layer, 1)])
                ext_f[layer, pl.ds(CONV_RADIUS + b * Q_LAT, Q_LAT), own] = z.reshape(shape)

            @pl.when(b0 == 0)
            def _():
                for dy in (-1, 1):
                    start_f_edge(layer, dy)

            for b in both:
                start_f(layer, b)

        @pl.when(layer == 0)
        def _():
            load(4, 0).wait()
            load(6, 0).wait()
        load(5, layer).wait()
        load(7, layer).wait()
        for dy in (-1, 1):
            given(-dy, lambda: copy_f(layer, "ns", dy, 0).wait_recv())

        @pl.loop(0, tiles)
        def _(k):
            t = lax.rem(k + 1, tiles)
            for dx, tile in ((-1, tiles - 1), (1, 0)):
                @pl.when(t == tile)
                def _():
                    for b in range(bands):
                        copy_f(layer, "ew", 0, dx, b).wait_recv()
                    for dy in (-1, 1):
                        given(-dy, lambda: copy_f(layer, "corner", dy, dx).wait_recv())
            x = ext_f[layer, :, pl.ds(per * t, per + 2)].reshape(-1, channels)
            nhat[...] = dot(forward[...], x).astype(BF16)

            @pl.loop(0, units // CHUNK)
            def _(c):
                lanes = pl.ds(pl.multiple_of(c * CHUNK, CHUNK), CHUNK)
                z = dot(nhat[...], expand[layer, :, lanes]).astype(BF16)
                re, im = z[:half], z[half:]
                k_re, k_im = khat[layer, :half, lanes], khat[layer, half:, lanes]
                y = jnp.concatenate([re * k_re - im * k_im, re * k_im + im * k_re], axis=0)
                act[:, lanes] = gelu(dot(inverse[...], y)).astype(BF16)

            cs = pl.ds(per * t, per)
            y = dot(act[...], shrink[layer]) + stream[:, cs].reshape(height * Q_LON, channels)
            shape = (height, per, COLS, channels)

            @pl.when(layer < layers - 1)
            def _():
                stream[:, cs] = y.reshape(shape)
                norm_tile(layer + 1, t, y)
                start_a(layer + 1, t)

            @pl.when(layer == layers - 1)
            def _():
                raw[:, cs] = y.astype(BF16).reshape(shape)
                pltpu.make_async_copy(raw.at[:, cs], out_hbm.at[:, cs], out_sem.at[t]).start()

    for t in range(tiles):
        cs = pl.ds(per * t, per)
        pltpu.make_async_copy(raw.at[:, cs], out_hbm.at[:, cs], out_sem.at[t]).wait()
    for layer in range(layers):
        wait_send_a(layer)
        wait_send_f(layer)


def per_device(
    state,
    attention_in,
    attention_out,
    expand_weight,
    depth_kernel,
    shrink_weight,
    norm_attention,
    norm_feedforward,
):
    height, width, channels = state.shape
    layers, side, _, units = depth_kernel.shape
    blocks = width // COLS
    tiles, bands = width // Q_LON, height // Q_LAT
    forward, basis, inverse = spectral(height, Q_LON, layers)
    taps = depth_kernel.transpose(1, 2, 0, 3)
    heavy = (
        attention_in, attention_out, expand_weight, shrink_weight, taps,
        jnp.asarray(forward), jnp.asarray(basis), jnp.asarray(inverse),
    )
    any_spec = pl.BlockSpec(memory_space=pl.ANY)
    vmem_spec = pl.BlockSpec(memory_space=pltpu.VMEM)
    shape = (height, blocks, COLS, channels)
    slots_a, slots_f = 2 * tiles + 6, 2 * bands + 6
    out = pl.pallas_call(
        kernel,
        out_shape=jax.ShapeDtypeStruct(shape, BF16),
        in_specs=[any_spec] + [vmem_spec] * 2 + [any_spec] * len(heavy),
        out_specs=any_spec,
        scratch_shapes=[pltpu.VMEM(a.shape, BF16) for a in heavy]
        + [
            pltpu.VMEM(shape, BF16),
            pltpu.VMEM((layers, height + 2 * RADIUS, blocks + 2, COLS, channels), BF16),
            pltpu.VMEM((layers, height + 2 * CONV_RADIUS, blocks + 2, COLS, channels), BF16),
            pltpu.VMEM(shape, F32),
            pltpu.VMEM(shape, BF16),
            pltpu.VMEM((height + 2 * RADIUS, blocks + 2, COLS, 2 * channels), BF16),
            pltpu.VMEM((2, Q_LAT, blocks, COLS, channels), BF16),
            pltpu.VMEM((bands, Q_LAT * Q_LON, K_LAT * K_LON), F32),
            pltpu.VMEM((forward.shape[0], channels), BF16),
            pltpu.VMEM((layers, forward.shape[0], units), BF16),
            pltpu.VMEM((height * Q_LON, units), BF16),
            pltpu.SemaphoreType.DMA((len(heavy), layers)),
            pltpu.SemaphoreType.DMA,
            pltpu.SemaphoreType.DMA((tiles,)),
            pltpu.SemaphoreType.DMA((layers, slots_a)),
            pltpu.SemaphoreType.DMA((layers, slots_a)),
            pltpu.SemaphoreType.DMA((layers, slots_f)),
            pltpu.SemaphoreType.DMA((layers, slots_f)),
        ],
        compiler_params=pltpu.CompilerParams(
            vmem_limit_bytes=VMEM_LIMIT, collective_id=0, has_side_effects=True
        ),
        name="blocks",
    )(
        state.reshape(shape), norm_attention, norm_feedforward, *heavy
    )
    return out.reshape(height, width, channels)


def solution(mesh):
    in_specs = (P("lat", "lon", None), P(), P(), P(), P(), P(), P(), P())
    out_specs = P("lat", "lon", None)
    return jax.shard_map(
        per_device, mesh=mesh, in_specs=in_specs, out_specs=out_specs, check_vma=False
    )
```

```python
import functools
import math

import jax
import jax.numpy as jnp
import numpy as np
from jax import lax
from jax.experimental import pallas as pl
from jax.experimental.pallas import tpu as pltpu
from jax.sharding import PartitionSpec as P

HEAD_DIM = 64
RADIUS = 6
CONV_RADIUS = 3
Q_LAT = 4
Q_LON = 16
COLS = 8
K_LAT = Q_LAT + 2 * RADIUS
K_LON = Q_LON + 2 * COLS
GROUP = 4
SPAN = GROUP * HEAD_DIM
CHUNK = 2048
NEG = -1e30
VMEM_LIMIT = 60 * 1024 * 1024
F32 = jnp.float32
BF16 = jnp.bfloat16
MESH = pl.DeviceIdType.MESH


def spectral(height, cols, layers):
    side = 2 * CONV_RADIUS + 1
    tall, wide = height + side - 1, cols + side - 1
    window, offset = cols + 2 * COLS, COLS - CONV_RADIUS
    kept = []
    for u in range(tall):
        for v in range(wide):
            other = ((-u) % tall, (-v) % wide)
            if (u, v) <= other:
                kept.append((u, v, (u, v) == other))
    m = len(kept)
    half = -(-m // 16) * 16
    u, v = (np.array([k[i] for k in kept], np.float64)[:, None] for i in (0, 1))
    single = np.array([k[2] for k in kept])[:, None]

    def phase(rows, columns, stride=None):
        r, c = np.meshgrid(np.arange(rows), columns, indexing="ij")
        return 2 * np.pi * (u * r.reshape(1, -1) / tall + v * c.reshape(1, -1) / wide)

    columns = np.arange(window) - offset
    inside = np.tile((columns >= 0) & (columns < wide), tall)[None]
    angle = phase(tall, columns)
    forward = np.zeros((2 * half, tall * window))
    forward[:m] = np.cos(angle) * inside
    forward[half : half + m] = -np.sin(angle) * inside * ~single
    angle = phase(side, np.arange(side))
    taps = np.zeros((layers, 2 * half, -(-side * side * layers // 16) * 16))
    for layer in range(layers):
        mine = slice(layer, side * side * layers, layers)
        taps[layer, :m, mine] = np.cos(angle)
        taps[layer, half : half + m, mine] = np.sin(angle) * ~single
    angle = phase(height, np.arange(cols))
    scale = np.where(single, 1.0, 2.0) / (tall * wide)
    inverse = np.zeros((height * cols, 2 * half))
    inverse[:, :m] = (np.cos(angle) * scale).T
    inverse[:, half : half + m] = -(np.sin(angle) * scale).T
    coarse = taps.astype(jnp.bfloat16)
    fine = (taps - coarse.astype(np.float64)).astype(jnp.bfloat16)
    return (
        forward.astype(jnp.bfloat16),
        np.concatenate([coarse, fine], axis=2),
        inverse.astype(jnp.bfloat16),
    )


def norm_rows(stream, gain):
    average = jnp.mean(stream, axis=-1, keepdims=True)
    centred = stream - average
    spread = jnp.mean(centred * centred, axis=-1, keepdims=True)
    return (centred * lax.rsqrt(spread + 1e-05) * gain).astype(BF16)


def gelu(x):
    return 0.5 * x * (1.0 + lax.erf(x * math.sqrt(0.5)))


def dot(a, b):
    return jnp.dot(a, b, preferred_element_type=F32)


def kernel(
    state_ref, gain_a_ref, gain_f_ref,
    w_in_hbm, w_out_hbm, expand_hbm, shrink_hbm, taps_hbm, forward_hbm, basis_hbm, inverse_hbm,
    out_ref,
    w_in, w_out, expand, shrink, taps, forward, basis, inverse,
    ext_a, ext_f, stream, q_ref, kv_ref, mixed_ref, bias_ref, nhat, khat, act,
    load_sem, send_a, recv_a, send_f, recv_f,
):
    height, blocks, _, channels = state_ref.shape
    width = blocks * COLS
    layers = w_in.shape[0]
    units = expand.shape[2]
    tiles = width // Q_LON
    per = Q_LON // COLS
    bands = height // Q_LAT
    half = forward.shape[0] // 2
    part = Q_LAT * Q_LON
    keys = K_LAT * K_LON

    lat, lon = lax.axis_index("lat"), lax.axis_index("lon")
    n_lat, n_lon = lax.axis_size("lat"), lax.axis_size("lon")
    east, west = lax.rem(lon + 1, n_lon), lax.rem(lon + n_lon - 1, n_lon)
    has = {-1: lat > 0, 1: lat < n_lat - 1}

    def peer(dy, dx):
        return {"lat": lat + dy, "lon": {-1: west, 0: lon, 1: east}[dx]}

    def given(dy, f):
        if dy == 0:
            f()
        else:
            pl.when(has[dy])(f)

    loads = {}
    plan = [(w_in, w_in_hbm, True), (taps, taps_hbm, False), (basis, basis_hbm, True),
            (w_out, w_out_hbm, True), (forward, forward_hbm, False), (expand, expand_hbm, True),
            (inverse, inverse_hbm, False), (shrink, shrink_hbm, True)]
    spot = 0
    for layer in range(layers):
        for i, (dst, src, layered) in enumerate(plan):
            if layered or layer == 0:
                view = (src.at[layer], dst.at[layer]) if layered else (src, dst)
                loads[i, layer] = pltpu.make_async_copy(*view, load_sem.at[spot])
                loads[i, layer].start()
                spot += 1

    def ready(i, layer):
        loads[i, layer].wait()

    def transfer(buf, reach, send, recv, slot, dy, dx, rows, cols):
        r0, rn = rows
        c0, cn = cols
        to_r = r0 - dy * height
        to_c = c0 - dx * blocks
        return pltpu.make_async_remote_copy(
            src_ref=buf.at[pl.ds(reach + r0, rn), pl.ds(1 + c0, cn)],
            dst_ref=buf.at[pl.ds(reach + to_r, rn), pl.ds(1 + to_c, cn)],
            send_sem=send.at[slot],
            recv_sem=recv.at[slot],
            device_id=peer(dy, dx),
            device_id_type=MESH,
        )

    def edge(dy, reach):
        return (0, reach) if dy < 0 else (height - reach, reach)

    def column(dx):
        return (0, 1) if dx < 0 else (blocks - 1, 1)

    def copy_a(layer, kind, dy, dx, t=0):
        buf, send, recv = ext_a.at[layer], send_a.at[layer], recv_a.at[layer]
        if kind == "ns":
            slot = (tiles if dy > 0 else 0) + t
            return transfer(buf, RADIUS, send, recv, slot, dy, 0, edge(dy, RADIUS), (per * t, per))
        if kind == "ew":
            slot = 2 * tiles + (dx > 0)
            return transfer(buf, RADIUS, send, recv, slot, 0, dx, (0, height), column(dx))
        slot = 2 * tiles + 2 + 2 * (dy > 0) + (dx > 0)
        return transfer(buf, RADIUS, send, recv, slot, dy, dx, edge(dy, RADIUS), column(dx))

    def copy_f(layer, kind, dy, dx, b=0):
        buf, send, recv = ext_f.at[layer], send_f.at[layer], recv_f.at[layer]
        if kind == "ns":
            return transfer(
                buf, CONV_RADIUS, send, recv, int(dy > 0), dy, 0, edge(dy, CONV_RADIUS), (0, blocks)
            )
        if kind == "ew":
            slot = 6 + (bands if dx > 0 else 0) + b
            return transfer(
                buf, CONV_RADIUS, send, recv, slot, 0, dx, (Q_LAT * b, Q_LAT), column(dx)
            )
        slot = 2 + 2 * (dy > 0) + (dx > 0)
        return transfer(buf, CONV_RADIUS, send, recv, slot, dy, dx, edge(dy, CONV_RADIUS), column(dx))

    def start_a(layer, t):
        for dy in (-1, 1):
            given(dy, lambda dy=dy: copy_a(layer, "ns", dy, 0, t).start())
        for dx, tile in ((-1, 0), (1, tiles - 1)):
            @pl.when(t == tile)
            def _():
                copy_a(layer, "ew", 0, dx).start()
                for dy in (-1, 1):
                    given(dy, lambda dy=dy: copy_a(layer, "corner", dy, dx).start())

    def wait_recv_a(layer, what):
        if what == "ew":
            for dx in (-1, 1):
                copy_a(layer, "ew", 0, dx).wait_recv()
        else:
            for dy in (-1, 1):
                def _():
                    for t in range(tiles):
                        copy_a(layer, "ns", dy, 0, t).wait_recv()
                    for dx in (-1, 1):
                        copy_a(layer, "corner", dy, dx).wait_recv()
                given(-dy, _)

    def wait_send_a(layer):
        for dx in (-1, 1):
            copy_a(layer, "ew", 0, dx).wait_send()
        for dy in (-1, 1):
            def _():
                for t in range(tiles):
                    copy_a(layer, "ns", dy, 0, t).wait_send()
                for dx in (-1, 1):
                    copy_a(layer, "corner", dy, dx).wait_send()
            given(dy, _)

    def start_f(layer, b):
        for dx in (-1, 1):
            copy_f(layer, "ew", 0, dx, b).start()

    def start_f_edge(layer, dy):
        def _():
            copy_f(layer, "ns", dy, 0).start()
            for dx in (-1, 1):
                copy_f(layer, "corner", dy, dx).start()
        given(dy, _)

    def wait_send_f(layer):
        for dx in (-1, 1):
            for b in range(bands):
                copy_f(layer, "ew", 0, dx, b).wait_send()
        for dy in (-1, 1):
            def _():
                copy_f(layer, "ns", dy, 0).wait_send()
                for dx in (-1, 1):
                    copy_f(layer, "corner", dy, dx).wait_send()
            given(dy, _)

    barrier = pltpu.get_barrier_semaphore()
    for dy in (-1, 0, 1):
        for dx in (-1, 0, 1):
            if (dy, dx) != (0, 0):
                given(dy, lambda dy=dy, dx=dx: pl.semaphore_signal(
                    barrier, inc=1, device_id=peer(dy, dx), device_id_type=MESH))

    def norm_tile(layer, t, x):
        z = norm_rows(x, gain_a_ref[layer : layer + 1]).reshape(height, per, COLS, channels)
        ext_a[layer, pl.ds(RADIUS, height), pl.ds(1 + per * t, per)] = z

    pl.semaphore_wait(barrier, 2 + 3 * sum(h.astype(jnp.int32) for h in has.values()))

    @pl.loop(0, tiles)
    def _(t):
        x = state_ref[:, pl.ds(per * t, per)].astype(F32)
        stream[:, pl.ds(per * t, per)] = x
        norm_tile(0, t, x.reshape(height * Q_LON, channels))
        start_a(0, t)

    for dy in (-1, 1):
        @pl.when(jnp.logical_not(has[dy]))
        def _():
            for buf, reach in ((ext_a, RADIUS), (ext_f, CONV_RADIUS)):
                first = 0 if dy < 0 else reach + height
                shape = (layers, reach) + buf.shape[2:]
                buf[:, first : first + reach] = jnp.zeros(shape, BF16)

    m = lax.broadcasted_iota(jnp.int32, (part, keys), 0)
    n = lax.broadcasted_iota(jnp.int32, (part, keys), 1)
    up = n // K_LON - RADIUS - m // Q_LON
    over = n % K_LON - COLS - m % Q_LON
    near = (jnp.abs(up) <= RADIUS) & (jnp.abs(over) <= RADIUS)

    @pl.loop(0, bands)
    def _(b):
        place = lat * height + b * Q_LAT + n // K_LON - RADIUS
        bias_ref[b] = jnp.where(near & (place >= 0) & (place < n_lat * height), 0.0, NEG)

    ready(1, 0)
    for layer in range(layers):
        ready(2, layer)

    @pl.loop(0, units // CHUNK)
    def _(c):
        lanes = pl.ds(pl.multiple_of(c * CHUNK, CHUNK), CHUNK)
        x = taps[:, :, :, lanes].astype(F32).reshape(-1, CHUNK)
        fill = jnp.zeros((basis.shape[2] // 2 - x.shape[0], CHUNK), F32)
        x = jnp.concatenate([x, fill], axis=0).astype(BF16)
        x = jnp.concatenate([x, x], axis=0)
        for layer in range(layers):
            khat[layer, :, lanes] = dot(basis[layer], x).astype(BF16)

    lane_head = lax.broadcasted_iota(jnp.int32, (part, SPAN), 1) // HEAD_DIM

    def attend(r0, t, g, bias):
        lo = g * SPAN
        rows, cols = pl.ds(r0, K_LAT), slice(per * t, per * t + K_LON // COLS)
        q = q_ref[pl.ds(r0, Q_LAT), per * t : per * t + per, :, lo : lo + SPAN].reshape(part, SPAN)
        k = kv_ref[rows, cols, :, lo : lo + SPAN].reshape(keys, SPAN)
        v = kv_ref[rows, cols, :, channels + lo : channels + lo + SPAN].reshape(keys, SPAN)
        qq = jnp.concatenate(
            [jnp.where(lane_head == h, q, jnp.zeros_like(q)) for h in range(GROUP)], axis=0
        )
        s = lax.dot_general(qq, k, (((1,), (1,)), ((), ())), preferred_element_type=F32)
        s = (s.reshape(GROUP, part, keys) + bias[None]).reshape(s.shape)
        e = jnp.exp(s - jnp.max(s, axis=-1, keepdims=True))
        total = jnp.sum(e, axis=-1, keepdims=True)
        o = dot(e.astype(BF16), v) * (1.0 / total)
        m = jnp.zeros((part, SPAN), F32)
        for h in range(GROUP):
            m = jnp.where(lane_head == h, o[h * part : (h + 1) * part], m)
        mixed_ref[:, per * t : per * t + per, :, lo : lo + SPAN] = m.astype(BF16).reshape(
            Q_LAT, per, COLS, SPAN
        )

    def band(layer, b):
        r0 = b * Q_LAT
        for t in range(tiles):
            for g in range(channels // SPAN):
                attend(r0, t, g, bias_ref[b])
        rs = pl.ds(r0, Q_LAT)
        x = mixed_ref[...].reshape(Q_LAT * width, channels)
        y = dot(x, w_out[layer]) + stream[rs].reshape(Q_LAT * width, channels)
        shape = (Q_LAT, blocks, COLS, channels)
        stream[rs] = y.reshape(shape)
        z = norm_rows(y, gain_f_ref[layer : layer + 1])
        ext_f[layer, pl.ds(CONV_RADIUS + r0, Q_LAT), 1 : 1 + blocks] = z.reshape(shape)
        start_f(layer, b)

    reach_b = -(-RADIUS // Q_LAT)
    own = slice(1, 1 + blocks)

    def project(layer, rows, cols, count):
        x = ext_a[layer, rows, cols].reshape(-1, channels)
        y = dot(x, w_in[layer, :, channels:]).astype(BF16)
        kv_ref[rows, cols] = y.reshape(y.shape[0] // (count * COLS), count, COLS, 2 * channels)

    for layer in range(layers):
        last = layer == layers - 1
        ready(0, layer)
        x = ext_a[layer, RADIUS : RADIUS + height, own].reshape(height * width, channels)
        shape = (height, blocks, COLS, channels)
        y = dot(x, w_in[layer, :, :channels]).astype(BF16) * (1.0 / math.sqrt(HEAD_DIM))
        q_ref[...] = y.astype(BF16).reshape(shape)
        for i in range(2):
            cs = slice((i + 1) * channels, (i + 2) * channels)
            y = dot(x, w_in[layer, :, cs]).astype(BF16)
            to = slice(i * channels, (i + 1) * channels)
            kv_ref[RADIUS : RADIUS + height, own, :, to] = y.reshape(shape)
        wait_recv_a(layer, "ew")
        for c in (0, 1 + blocks):
            project(layer, slice(RADIUS, RADIUS + height), slice(c, c + 1), 1)
        ready(3, layer)

        @pl.loop(reach_b, bands - reach_b)
        def _(b):
            band(layer, b)

        wait_recv_a(layer, "rest")
        for r in (0, RADIUS + height):
            project(layer, slice(r, r + RADIUS), slice(0, blocks + 2), blocks + 2)

        for j in range(reach_b):
            @pl.loop(0, 2)
            def _(k):
                band(layer, j + k * (bands - 1 - 2 * j))
                if j == 0:
                    for i, dy in enumerate((-1, 1)):
                        @pl.when(k == i)
                        def _():
                            start_f_edge(layer, dy)

        if layer == 0:
            ready(4, 0)
            ready(6, 0)
        ready(5, layer)
        ready(7, layer)
        for dy in (-1, 1):
            given(-dy, lambda: copy_f(layer, "ns", dy, 0).wait_recv())

        @pl.loop(0, tiles)
        def _(k):
            t = lax.rem(k + 1, tiles)
            for dx, tile in ((-1, tiles - 1), (1, 0)):
                @pl.when(t == tile)
                def _():
                    for b in range(bands):
                        copy_f(layer, "ew", 0, dx, b).wait_recv()
                    for dy in (-1, 1):
                        given(-dy, lambda: copy_f(layer, "corner", dy, dx).wait_recv())
            x = ext_f[layer, :, pl.ds(per * t, per + 2)].reshape(-1, channels)
            nhat[...] = dot(forward[...], x).astype(BF16)

            @pl.loop(0, units // CHUNK)
            def _(c):
                lanes = pl.ds(pl.multiple_of(c * CHUNK, CHUNK), CHUNK)
                z = dot(nhat[...], expand[layer, :, lanes]).astype(BF16)
                re, im = z[:half], z[half:]
                k_re, k_im = khat[layer, :half, lanes], khat[layer, half:, lanes]
                y = jnp.concatenate([re * k_re - im * k_im, re * k_im + im * k_re], axis=0)
                act[:, lanes] = gelu(dot(inverse[...], y)).astype(BF16)

            cs = pl.ds(per * t, per)
            y = dot(act[...], shrink[layer]) + stream[:, cs].reshape(height * Q_LON, channels)
            shape = (height, per, COLS, channels)
            if last:
                out_ref[:, cs] = y.astype(BF16).reshape(shape)
            else:
                stream[:, cs] = y.reshape(shape)
                norm_tile(layer + 1, t, y)
                start_a(layer + 1, t)

    for layer in range(layers):
        wait_send_a(layer)
        wait_send_f(layer)


def per_device(
    state,
    attention_in,
    attention_out,
    expand_weight,
    depth_kernel,
    shrink_weight,
    norm_attention,
    norm_feedforward,
):
    height, width, channels = state.shape
    layers, side, _, units = depth_kernel.shape
    blocks = width // COLS
    tiles, bands = width // Q_LON, height // Q_LAT
    forward, basis, inverse = spectral(height, Q_LON, layers)
    taps = depth_kernel.transpose(1, 2, 0, 3)
    heavy = (
        attention_in, attention_out, expand_weight, shrink_weight, taps,
        jnp.asarray(forward), jnp.asarray(basis), jnp.asarray(inverse),
    )
    any_spec = pl.BlockSpec(memory_space=pl.ANY)
    vmem_spec = pl.BlockSpec(memory_space=pltpu.VMEM)
    shape = (height, blocks, COLS, channels)
    slots_a, slots_f = 2 * tiles + 6, 2 * bands + 6
    out = pl.pallas_call(
        kernel,
        out_shape=jax.ShapeDtypeStruct(shape, BF16),
        in_specs=[vmem_spec] * 3 + [any_spec] * len(heavy),
        out_specs=vmem_spec,
        scratch_shapes=[pltpu.VMEM(a.shape, BF16) for a in heavy]
        + [
            pltpu.VMEM((layers, height + 2 * RADIUS, blocks + 2, COLS, channels), BF16),
            pltpu.VMEM((layers, height + 2 * CONV_RADIUS, blocks + 2, COLS, channels), BF16),
            pltpu.VMEM(shape, F32),
            pltpu.VMEM(shape, BF16),
            pltpu.VMEM((height + 2 * RADIUS, blocks + 2, COLS, 2 * channels), BF16),
            pltpu.VMEM((Q_LAT, blocks, COLS, channels), BF16),
            pltpu.VMEM((bands, Q_LAT * Q_LON, K_LAT * K_LON), F32),
            pltpu.VMEM((forward.shape[0], channels), BF16),
            pltpu.VMEM((layers, forward.shape[0], units), BF16),
            pltpu.VMEM((height * Q_LON, units), BF16),
            pltpu.SemaphoreType.DMA((5 * layers + 3,)),
            pltpu.SemaphoreType.DMA((layers, slots_a)),
            pltpu.SemaphoreType.DMA((layers, slots_a)),
            pltpu.SemaphoreType.DMA((layers, slots_f)),
            pltpu.SemaphoreType.DMA((layers, slots_f)),
        ],
        compiler_params=pltpu.CompilerParams(
            vmem_limit_bytes=VMEM_LIMIT, collective_id=0, has_side_effects=True
        ),
        name="blocks",
    )(
        state.reshape(shape), norm_attention, norm_feedforward, *heavy
    )
    return out.reshape(height, width, channels)


def solution(mesh):
    in_specs = (P("lat", "lon", None), P(), P(), P(), P(), P(), P(), P())
    out_specs = P("lat", "lon", None)
    return jax.shard_map(
        per_device, mesh=mesh, in_specs=in_specs, out_specs=out_specs, check_vma=False
    )
```

```python
import functools
import math

import jax
import jax.numpy as jnp
import numpy as np
from jax import lax
from jax.experimental import pallas as pl
from jax.experimental.pallas import tpu as pltpu
from jax.sharding import PartitionSpec as P

HEAD_DIM = 64
RADIUS = 6
CONV_RADIUS = 3
Q_LAT = 4
Q_LON = 16
COLS = 8
K_LAT = Q_LAT + 2 * RADIUS
K_LON = Q_LON + 2 * COLS
GROUP = 4
SPAN = GROUP * HEAD_DIM
CHUNK = 2048
NEG = -1e30
VMEM_LIMIT = 60 * 1024 * 1024
F32 = jnp.float32
BF16 = jnp.bfloat16
MESH = pl.DeviceIdType.MESH


def spectral(height, cols, layers):
    side = 2 * CONV_RADIUS + 1
    tall, wide = height + side - 1, cols + side - 1
    window, offset = cols + 2 * COLS, COLS - CONV_RADIUS
    kept = []
    for u in range(tall):
        for v in range(wide):
            other = ((-u) % tall, (-v) % wide)
            if (u, v) <= other:
                kept.append((u, v, (u, v) == other))
    m = len(kept)
    half = -(-m // 16) * 16
    u, v = (np.array([k[i] for k in kept], np.float64)[:, None] for i in (0, 1))
    single = np.array([k[2] for k in kept])[:, None]

    def phase(rows, columns, stride=None):
        r, c = np.meshgrid(np.arange(rows), columns, indexing="ij")
        return 2 * np.pi * (u * r.reshape(1, -1) / tall + v * c.reshape(1, -1) / wide)

    columns = np.arange(window) - offset
    inside = np.tile((columns >= 0) & (columns < wide), tall)[None]
    angle = phase(tall, columns)
    forward = np.zeros((2 * half, tall * window))
    forward[:m] = np.cos(angle) * inside
    forward[half : half + m] = -np.sin(angle) * inside * ~single
    angle = phase(side, np.arange(side))
    taps = np.zeros((layers, 2 * half, -(-side * side * layers // 16) * 16))
    for layer in range(layers):
        mine = slice(layer, side * side * layers, layers)
        taps[layer, :m, mine] = np.cos(angle)
        taps[layer, half : half + m, mine] = np.sin(angle) * ~single
    angle = phase(height, np.arange(cols))
    scale = np.where(single, 1.0, 2.0) / (tall * wide)
    inverse = np.zeros((height * cols, 2 * half))
    inverse[:, :m] = (np.cos(angle) * scale).T
    inverse[:, half : half + m] = -(np.sin(angle) * scale).T
    coarse = taps.astype(jnp.bfloat16)
    fine = (taps - coarse.astype(np.float64)).astype(jnp.bfloat16)
    return (
        forward.astype(jnp.bfloat16),
        np.concatenate([coarse, fine], axis=2),
        inverse.astype(jnp.bfloat16),
    )


def norm_rows(stream, gain):
    average = jnp.mean(stream, axis=-1, keepdims=True)
    centred = stream - average
    spread = jnp.mean(centred * centred, axis=-1, keepdims=True)
    return (centred * lax.rsqrt(spread + 1e-05) * gain).astype(BF16)


def gelu(x):
    return 0.5 * x * (1.0 + lax.erf(x * math.sqrt(0.5)))


def dot(a, b):
    return jnp.dot(a, b, preferred_element_type=F32)


def kernel(
    state_hbm, gain_a_ref, gain_f_ref,
    w_in_hbm, w_out_hbm, expand_hbm, shrink_hbm, taps_hbm, forward_hbm, basis_hbm, inverse_hbm,
    out_hbm,
    w_in, w_out, expand, shrink, taps, forward, basis, inverse,
    raw, ext_a, ext_f, stream, q_ref, kv_ref, mixed_ref, bias_ref, nhat, khat, act,
    hop, hop_recv, hop_send, load_sem, state_sem, out_sem, send_a, recv_a, send_f, recv_f,
):
    height, blocks, _, channels = raw.shape
    width = blocks * COLS
    layers = w_in.shape[0]
    units = expand.shape[2]
    tiles = width // Q_LON
    per = Q_LON // COLS
    bands = height // Q_LAT
    half = forward.shape[0] // 2
    part = Q_LAT * Q_LON
    keys = K_LAT * K_LON

    lat, lon = lax.axis_index("lat"), lax.axis_index("lon")
    n_lat, n_lon = lax.axis_size("lat"), lax.axis_size("lon")
    east, west = lax.rem(lon + 1, n_lon), lax.rem(lon + n_lon - 1, n_lon)
    has = {-1: lat > 0, 1: lat < n_lat - 1}

    def peer(dy, dx):
        return {"lat": lat + dy, "lon": {-1: west, 0: lon, 1: east}[dx]}

    odd = lax.rem(lat, 2) == 1
    even = jnp.logical_not(odd)
    paired = n_lat % 2 == 0
    far = {-1: lat >= 2, 1: lat <= n_lat - 3}
    detours = {-1: even & has[-1], 1: odd & has[1]}
    relays = {-1: even & far[1], 1: odd & far[-1]}

    def given(dy, f):
        if dy == 0:
            f()
        else:
            pl.when(has[dy])(f)

    plan = [(w_in, w_in_hbm, True), (taps, taps_hbm, False), (basis, basis_hbm, True),
            (w_out, w_out_hbm, True), (forward, forward_hbm, False), (expand, expand_hbm, True),
            (inverse, inverse_hbm, False), (shrink, shrink_hbm, True)]

    def load(i, layer):
        dst, src, layered = plan[i]
        view = (src.at[layer], dst.at[layer]) if layered else (src, dst)
        return pltpu.make_async_copy(*view, load_sem.at[i, layer])

    def transfer(buf, reach, send, recv, slot, dy, dx, rows, cols):
        r0, rn = rows
        c0, cn = cols
        to_r = r0 - dy * height
        to_c = c0 - dx * blocks
        return pltpu.make_async_remote_copy(
            src_ref=buf.at[pl.ds(reach + r0, rn), pl.ds(1 + c0, cn)],
            dst_ref=buf.at[pl.ds(reach + to_r, rn), pl.ds(1 + to_c, cn)],
            send_sem=send.at[slot],
            recv_sem=recv.at[slot],
            device_id=peer(dy, dx),
            device_id_type=MESH,
        )

    def edge(dy, reach):
        return (0, reach) if dy < 0 else (height - reach, reach)

    def column(dx):
        return (0, 1) if dx < 0 else (blocks - 1, 1)

    def copy_a(layer, kind, dy, dx, t=0):
        buf, send, recv = ext_a.at[layer], send_a.at[layer], recv_a.at[layer]
        if kind == "ns":
            slot = (tiles if dy > 0 else 0) + t
            return transfer(buf, RADIUS, send, recv, slot, dy, 0, edge(dy, RADIUS), (per * t, per))
        if kind == "ew":
            slot = 2 * tiles + (dx > 0)
            return transfer(buf, RADIUS, send, recv, slot, 0, dx, (0, height), column(dx))
        slot = 2 * tiles + 2 + 2 * (dy > 0) + (dx > 0)
        return transfer(buf, RADIUS, send, recv, slot, dy, dx, edge(dy, RADIUS), column(dx))

    def copy_f(layer, kind, dy, dx, b=0):
        buf, send, recv = ext_f.at[layer], send_f.at[layer], recv_f.at[layer]
        if kind == "ns":
            return transfer(
                buf, CONV_RADIUS, send, recv, int(dy > 0), dy, 0, edge(dy, CONV_RADIUS), (0, blocks)
            )
        if kind == "ew":
            slot = 6 + (bands if dx > 0 else 0) + b
            return transfer(
                buf, CONV_RADIUS, send, recv, slot, 0, dx, (Q_LAT * b, Q_LAT), column(dx)
            )
        slot = 2 + 2 * (dy > 0) + (dx > 0)
        return transfer(buf, CONV_RADIUS, send, recv, slot, dy, dx, edge(dy, CONV_RADIUS), column(dx))

    detour = tiles - 1

    def hop_in(dy):
        r0, rn = edge(dy, RADIUS)
        return pltpu.make_async_remote_copy(
            src_ref=ext_a.at[0, pl.ds(RADIUS + r0, rn), pl.ds(1 + per * detour, per)],
            dst_ref=hop,
            send_sem=send_a.at[0, (tiles if dy > 0 else 0) + detour],
            recv_sem=hop_recv,
            device_id={"lat": lat + 2 * dy, "lon": lon},
            device_id_type=MESH,
        )

    def hop_out(dy):
        r0, rn = edge(dy, RADIUS)
        return pltpu.make_async_remote_copy(
            src_ref=hop,
            dst_ref=ext_a.at[0, pl.ds(RADIUS + r0 - dy * height, rn), pl.ds(1 + per * detour, per)],
            send_sem=hop_send,
            recv_sem=recv_a.at[0, (tiles if dy > 0 else 0) + detour],
            device_id={"lat": lat - dy, "lon": lon},
            device_id_type=MESH,
        )

    def start_first(dy, t):
        if t != detour or not paired:
            copy_a(0, "ns", dy, 0, t).start()
        else:
            pl.when(detours[dy])(lambda: hop_in(dy).start())
            pl.when(jnp.logical_not(detours[dy]))(lambda: copy_a(0, "ns", dy, 0, t).start())

    def start_a(layer, t):
        for dy in (-1, 1):
            if isinstance(layer, int):
                given(dy, lambda dy=dy: start_first(dy, t))
            else:
                given(dy, lambda dy=dy: copy_a(layer, "ns", dy, 0, t).start())
        for dx, tile in ((-1, 0), (1, tiles - 1)):
            @pl.when(t == tile)
            def _():
                copy_a(layer, "ew", 0, dx).start()
                for dy in (-1, 1):
                    given(dy, lambda dy=dy: copy_a(layer, "corner", dy, dx).start())

    def wait_recv_a(layer, what):
        if what == "ew":
            for dx in (-1, 1):
                copy_a(layer, "ew", 0, dx).wait_recv()
        else:
            for dy in (-1, 1):
                def _():
                    for t in range(tiles):
                        copy_a(layer, "ns", dy, 0, t).wait_recv()
                    for dx in (-1, 1):
                        copy_a(layer, "corner", dy, dx).wait_recv()
                given(-dy, _)

    def wait_send_a(layer):
        for dx in (-1, 1):
            copy_a(layer, "ew", 0, dx).wait_send()
        for dy in (-1, 1):
            def _():
                for t in range(tiles):
                    copy_a(layer, "ns", dy, 0, t).wait_send()
                for dx in (-1, 1):
                    copy_a(layer, "corner", dy, dx).wait_send()
            given(dy, _)

    def start_f(layer, b):
        for dx in (-1, 1):
            copy_f(layer, "ew", 0, dx, b).start()

    def start_f_edge(layer, dy):
        def _():
            copy_f(layer, "ns", dy, 0).start()
            for dx in (-1, 1):
                copy_f(layer, "corner", dy, dx).start()
        given(dy, _)

    def wait_send_f(layer):
        for dx in (-1, 1):
            for b in range(bands):
                copy_f(layer, "ew", 0, dx, b).wait_send()
        for dy in (-1, 1):
            def _():
                copy_f(layer, "ns", dy, 0).wait_send()
                for dx in (-1, 1):
                    copy_f(layer, "corner", dy, dx).wait_send()
            given(dy, _)

    barrier = pltpu.get_barrier_semaphore()
    for dy in (-1, 0, 1):
        for dx in (-1, 0, 1):
            if (dy, dx) != (0, 0):
                given(dy, lambda dy=dy, dx=dx: pl.semaphore_signal(
                    barrier, inc=1, device_id=peer(dy, dx), device_id_type=MESH))
    if paired:
        for dy in (-1, 1):
            @pl.when(far[dy])
            def _():
                pl.semaphore_signal(
                    barrier, inc=1, device_id={"lat": lat + 2 * dy, "lon": lon}, device_id_type=MESH
                )

    state_copy = pltpu.make_async_copy(state_hbm, raw, state_sem)
    state_copy.start()

    def norm_tile(layer, t, x):
        z = norm_rows(x, gain_a_ref[pl.ds(layer, 1)]).reshape(height, per, COLS, channels)
        ext_a[layer, pl.ds(RADIUS, height), pl.ds(1 + per * t, per)] = z

    state_copy.wait()
    load(0, 0).start()

    @pl.loop(0, tiles)
    def _(t):
        x = raw[:, pl.ds(per * t, per)].astype(F32)
        stream[:, pl.ds(per * t, per)] = x
        norm_tile(0, t, x.reshape(height * Q_LON, channels))

    peers = 2 + 3 * sum(h.astype(jnp.int32) for h in has.values())
    if paired:
        peers = peers + sum(h.astype(jnp.int32) for h in far.values())
    pl.semaphore_wait(barrier, peers)

    for t in reversed(range(tiles)):
        start_a(0, t)

    load(1, 0).start()
    for layer in range(layers):
        load(2, layer).start()
    for i in range(3, len(plan)):
        load(i, 0).start()

    for dy in (-1, 1):
        @pl.when(jnp.logical_not(has[dy]))
        def _():
            for buf, reach in ((ext_a, RADIUS), (ext_f, CONV_RADIUS)):
                first = 0 if dy < 0 else reach + height
                shape = (layers, reach) + buf.shape[2:]
                buf[:, first : first + reach] = jnp.zeros(shape, BF16)

    m = lax.broadcasted_iota(jnp.int32, (part, keys), 0)
    n = lax.broadcasted_iota(jnp.int32, (part, keys), 1)
    up = n // K_LON - RADIUS - m // Q_LON
    over = n % K_LON - COLS - m % Q_LON
    near = (jnp.abs(up) <= RADIUS) & (jnp.abs(over) <= RADIUS)

    @pl.loop(0, bands)
    def _(b):
        place = lat * height + b * Q_LAT + n // K_LON - RADIUS
        bias_ref[b] = jnp.where(near & (place >= 0) & (place < n_lat * height), 0.0, NEG)

    def spectra():
        load(1, 0).wait()
        for layer in range(layers):
            load(2, layer).wait()

        @pl.loop(0, units // CHUNK)
        def _(c):
            lanes = pl.ds(pl.multiple_of(c * CHUNK, CHUNK), CHUNK)
            x = taps[:, :, :, lanes].astype(F32).reshape(-1, CHUNK)
            fill = jnp.zeros((basis.shape[2] // 2 - x.shape[0], CHUNK), F32)
            x = jnp.concatenate([x, fill], axis=0).astype(BF16)
            x = jnp.concatenate([x, x], axis=0)
            for layer in range(layers):
                khat[layer, :, lanes] = dot(basis[layer], x).astype(BF16)

        for layer in range(1, layers):
            for i, (_, _, layered) in enumerate(plan):
                if layered and i != 2:
                    load(i, layer).start()

    lane_head = lax.broadcasted_iota(jnp.int32, (part, SPAN), 1) // HEAD_DIM

    def attend(i, b, t, g):
        lo = g * SPAN
        rows, cols = pl.ds(b * Q_LAT, K_LAT), slice(per * t, per * t + K_LON // COLS)
        mine = slice(per * t, per * t + per)
        q = q_ref[pl.ds(b * Q_LAT, Q_LAT), mine, :, lo : lo + SPAN].reshape(part, SPAN)
        k = kv_ref[rows, cols, :, lo : lo + SPAN].reshape(keys, SPAN)
        v = kv_ref[rows, cols, :, channels + lo : channels + lo + SPAN].reshape(keys, SPAN)
        qq = jnp.concatenate(
            [jnp.where(lane_head == h, q, jnp.zeros_like(q)) for h in range(GROUP)], axis=0
        )
        s = lax.dot_general(qq, k, (((1,), (1,)), ((), ())), preferred_element_type=F32)
        s = (s.reshape(GROUP, part, keys) + bias_ref[b][None]).reshape(s.shape)
        e = jnp.exp(s - jnp.max(s, axis=-1, keepdims=True))
        total = jnp.sum(e, axis=-1, keepdims=True)
        o = dot(e.astype(BF16), v) * (1.0 / total)
        m = jnp.zeros((part, SPAN), F32)
        for h in range(GROUP):
            m = jnp.where(lane_head == h, o[h * part : (h + 1) * part], m)
        mixed_ref[i, :, mine, :, lo : lo + SPAN] = m.astype(BF16).reshape(Q_LAT, per, COLS, SPAN)

    own = slice(1, 1 + blocks)
    pairs = bands // 2

    def project(layer, rows, cols, count):
        x = ext_a[layer, rows, cols].reshape(-1, channels)
        y = dot(x, w_in[layer, :, channels:]).astype(BF16)
        kv_ref[rows, cols] = y.reshape(y.shape[0] // (count * COLS), count, COLS, 2 * channels)

    @pl.loop(0, layers)
    def _(layer):
        load(0, layer).wait()
        x = ext_a[layer, RADIUS : RADIUS + height, own].reshape(height * width, channels)
        shape = (height, blocks, COLS, channels)
        y = dot(x, w_in[layer, :, :channels]).astype(BF16) * (1.0 / math.sqrt(HEAD_DIM))
        q_ref[...] = y.astype(BF16).reshape(shape)
        for i in range(2):
            cs = slice((i + 1) * channels, (i + 2) * channels)
            y = dot(x, w_in[layer, :, cs]).astype(BF16)
            to = slice(i * channels, (i + 1) * channels)
            kv_ref[RADIUS : RADIUS + height, own, :, to] = y.reshape(shape)

        @pl.when(layer == 0)
        def _():
            if paired:
                for dy in (-1, 1):
                    @pl.when(relays[dy])
                    def _():
                        hop_in(dy).wait_recv()
                        hop_out(dy).start()
            spectra()

        @pl.loop(0, pairs)
        def _(p):
            b0 = lax.rem(p + pairs - 1, pairs)
            both = (b0, bands - 1 - b0)

            @pl.when(b0 == 0)
            def _():
                wait_recv_a(layer, "rest")
                for r in (0, RADIUS + height):
                    project(layer, slice(r, r + RADIUS), slice(0, blocks + 2), blocks + 2)

            for i, b in enumerate(both):
                for t in range(1, tiles - 1):
                    for g in range(channels // SPAN):
                        attend(i, b, t, g)

                if i == 0:
                    @pl.when(p == 0)
                    def _():
                        wait_recv_a(layer, "ew")
                        for c in (0, 1 + blocks):
                            project(layer, slice(RADIUS, RADIUS + height), slice(c, c + 1), 1)
                        load(3, layer).wait()

                for t in (0, tiles - 1):
                    for g in range(channels // SPAN):
                        attend(i, b, t, g)
                rs = pl.ds(b * Q_LAT, Q_LAT)
                shape = (Q_LAT, blocks, COLS, channels)
                y = dot(mixed_ref[i].reshape(Q_LAT * width, channels), w_out[layer])
                y = y + stream[rs].reshape(Q_LAT * width, channels)
                stream[rs] = y.reshape(shape)
                z = norm_rows(y, gain_f_ref[pl.ds(layer, 1)])
                ext_f[layer, pl.ds(CONV_RADIUS + b * Q_LAT, Q_LAT), own] = z.reshape(shape)

                @pl.when(b0 == 0)
                def _():
                    start_f_edge(layer, 2 * i - 1)

                start_f(layer, b)

        @pl.when(layer == 0)
        def _():
            load(4, 0).wait()
            load(6, 0).wait()
        load(5, layer).wait()
        load(7, layer).wait()
        for dy in (-1, 1):
            given(-dy, lambda: copy_f(layer, "ns", dy, 0).wait_recv())

        @pl.loop(0, tiles)
        def _(k):
            t = lax.rem(k + 1, tiles)
            for dx, tile in ((-1, tiles - 1), (1, 0)):
                @pl.when(t == tile)
                def _():
                    for b in range(bands):
                        copy_f(layer, "ew", 0, dx, b).wait_recv()
                    for dy in (-1, 1):
                        given(-dy, lambda: copy_f(layer, "corner", dy, dx).wait_recv())
            x = ext_f[layer, :, pl.ds(per * t, per + 2)].reshape(-1, channels)
            nhat[...] = dot(forward[...], x).astype(BF16)

            @pl.loop(0, units // CHUNK)
            def _(c):
                lanes = pl.ds(pl.multiple_of(c * CHUNK, CHUNK), CHUNK)
                z = dot(nhat[...], expand[layer, :, lanes]).astype(BF16)
                re, im = z[:half], z[half:]
                k_re, k_im = khat[layer, :half, lanes], khat[layer, half:, lanes]
                y = jnp.concatenate([re * k_re - im * k_im, re * k_im + im * k_re], axis=0)
                act[:, lanes] = gelu(dot(inverse[...], y)).astype(BF16)

            cs = pl.ds(per * t, per)
            y = dot(act[...], shrink[layer]) + stream[:, cs].reshape(height * Q_LON, channels)
            shape = (height, per, COLS, channels)

            @pl.when(layer < layers - 1)
            def _():
                stream[:, cs] = y.reshape(shape)
                norm_tile(layer + 1, t, y)
                start_a(layer + 1, t)

            @pl.when(layer == layers - 1)
            def _():
                raw[:, cs] = y.astype(BF16).reshape(shape)
                pltpu.make_async_copy(raw.at[:, cs], out_hbm.at[:, cs], out_sem.at[t]).start()

    for t in range(tiles):
        cs = pl.ds(per * t, per)
        pltpu.make_async_copy(raw.at[:, cs], out_hbm.at[:, cs], out_sem.at[t]).wait()
    if paired:
        for dy in (-1, 1):
            pl.when(relays[dy])(lambda: hop_out(dy).wait_send())
    for layer in range(layers):
        wait_send_a(layer)
        wait_send_f(layer)


def per_device(
    state,
    attention_in,
    attention_out,
    expand_weight,
    depth_kernel,
    shrink_weight,
    norm_attention,
    norm_feedforward,
):
    height, width, channels = state.shape
    layers, side, _, units = depth_kernel.shape
    blocks = width // COLS
    tiles, bands = width // Q_LON, height // Q_LAT
    forward, basis, inverse = spectral(height, Q_LON, layers)
    taps = depth_kernel.transpose(1, 2, 0, 3)
    heavy = (
        attention_in, attention_out, expand_weight, shrink_weight, taps,
        jnp.asarray(forward), jnp.asarray(basis), jnp.asarray(inverse),
    )
    any_spec = pl.BlockSpec(memory_space=pl.ANY)
    vmem_spec = pl.BlockSpec(memory_space=pltpu.VMEM)
    shape = (height, blocks, COLS, channels)
    slots_a, slots_f = 2 * tiles + 6, 2 * bands + 6
    out = pl.pallas_call(
        kernel,
        out_shape=jax.ShapeDtypeStruct(shape, BF16),
        in_specs=[any_spec] + [vmem_spec] * 2 + [any_spec] * len(heavy),
        out_specs=any_spec,
        scratch_shapes=[pltpu.VMEM(a.shape, BF16) for a in heavy]
        + [
            pltpu.VMEM(shape, BF16),
            pltpu.VMEM((layers, height + 2 * RADIUS, blocks + 2, COLS, channels), BF16),
            pltpu.VMEM((layers, height + 2 * CONV_RADIUS, blocks + 2, COLS, channels), BF16),
            pltpu.VMEM(shape, F32),
            pltpu.VMEM(shape, BF16),
            pltpu.VMEM((height + 2 * RADIUS, blocks + 2, COLS, 2 * channels), BF16),
            pltpu.VMEM((2, Q_LAT, blocks, COLS, channels), BF16),
            pltpu.VMEM((bands, Q_LAT * Q_LON, K_LAT * K_LON), F32),
            pltpu.VMEM((forward.shape[0], channels), BF16),
            pltpu.VMEM((layers, forward.shape[0], units), BF16),
            pltpu.VMEM((height * Q_LON, units), BF16),
            pltpu.VMEM((RADIUS, Q_LON // COLS, COLS, channels), BF16),
            pltpu.SemaphoreType.DMA,
            pltpu.SemaphoreType.DMA,
            pltpu.SemaphoreType.DMA((len(heavy), layers)),
            pltpu.SemaphoreType.DMA,
            pltpu.SemaphoreType.DMA((tiles,)),
            pltpu.SemaphoreType.DMA((layers, slots_a)),
            pltpu.SemaphoreType.DMA((layers, slots_a)),
            pltpu.SemaphoreType.DMA((layers, slots_f)),
            pltpu.SemaphoreType.DMA((layers, slots_f)),
        ],
        compiler_params=pltpu.CompilerParams(
            vmem_limit_bytes=VMEM_LIMIT, collective_id=0, has_side_effects=True
        ),
        name="blocks",
    )(
        state.reshape(shape), norm_attention, norm_feedforward, *heavy
    )
    return out.reshape(height, width, channels)


def solution(mesh):
    in_specs = (P("lat", "lon", None), P(), P(), P(), P(), P(), P(), P())
    out_specs = P("lat", "lon", None)
    return jax.shard_map(
        per_device, mesh=mesh, in_specs=in_specs, out_specs=out_specs, check_vma=False
    )
```

```python
import functools
import math

import jax
import jax.numpy as jnp
import numpy as np
from jax import lax
from jax.experimental import pallas as pl
from jax.experimental.pallas import tpu as pltpu
from jax.sharding import PartitionSpec as P

HEAD_DIM = 64
RADIUS = 6
CONV_RADIUS = 3
Q_LAT = 4
Q_LON = 16
COLS = 8
K_LAT = Q_LAT + 2 * RADIUS
K_LON = Q_LON + 2 * COLS
GROUP = 4
SPAN = GROUP * HEAD_DIM
CHUNK = 2048
NEG = -1e30
VMEM_LIMIT = 60 * 1024 * 1024
F32 = jnp.float32
BF16 = jnp.bfloat16
MESH = pl.DeviceIdType.MESH


def spectral(height, cols, layers):
    side = 2 * CONV_RADIUS + 1
    tall, wide = height + side - 1, cols + side - 1
    window, offset = cols + 2 * COLS, COLS - CONV_RADIUS
    kept = []
    for u in range(tall):
        for v in range(wide):
            other = ((-u) % tall, (-v) % wide)
            if (u, v) <= other:
                kept.append((u, v, (u, v) == other))
    m = len(kept)
    half = -(-m // 16) * 16
    u, v = (np.array([k[i] for k in kept], np.float64)[:, None] for i in (0, 1))
    single = np.array([k[2] for k in kept])[:, None]

    def phase(rows, columns, stride=None):
        r, c = np.meshgrid(np.arange(rows), columns, indexing="ij")
        return 2 * np.pi * (u * r.reshape(1, -1) / tall + v * c.reshape(1, -1) / wide)

    columns = np.arange(window) - offset
    inside = np.tile((columns >= 0) & (columns < wide), tall)[None]
    angle = phase(tall, columns)
    forward = np.zeros((2 * half, tall * window))
    forward[:m] = np.cos(angle) * inside
    forward[half : half + m] = -np.sin(angle) * inside * ~single
    angle = phase(side, np.arange(side))
    taps = np.zeros((layers, 2 * half, -(-side * side * layers // 16) * 16))
    for layer in range(layers):
        mine = slice(layer, side * side * layers, layers)
        taps[layer, :m, mine] = np.cos(angle)
        taps[layer, half : half + m, mine] = np.sin(angle) * ~single
    angle = phase(height, np.arange(cols))
    scale = np.where(single, 1.0, 2.0) / (tall * wide)
    inverse = np.zeros((height * cols, 2 * half))
    inverse[:, :m] = (np.cos(angle) * scale).T
    inverse[:, half : half + m] = -(np.sin(angle) * scale).T
    coarse = taps.astype(jnp.bfloat16)
    fine = (taps - coarse.astype(np.float64)).astype(jnp.bfloat16)
    return (
        forward.astype(jnp.bfloat16),
        np.concatenate([coarse, fine], axis=2),
        inverse.astype(jnp.bfloat16),
    )


def norm_rows(stream, gain):
    average = jnp.mean(stream, axis=-1, keepdims=True)
    centred = stream - average
    spread = jnp.mean(centred * centred, axis=-1, keepdims=True)
    return (centred * lax.rsqrt(spread + 1e-05) * gain).astype(BF16)


def gelu(x):
    return 0.5 * x * (1.0 + lax.erf(x * math.sqrt(0.5)))


def dot(a, b):
    return jnp.dot(a, b, preferred_element_type=F32)


def kernel(
    state_hbm, gain_a_ref, gain_f_ref,
    w_in_hbm, w_out_hbm, expand_hbm, shrink_hbm, taps_hbm, forward_hbm, basis_hbm, inverse_hbm,
    out_hbm,
    w_in, w_out, expand, shrink, taps, forward, basis, inverse,
    raw, ext_a, ext_f, stream, q_ref, kv_ref, mixed_ref, bias_ref, nhat, khat, act,
    hop, hop_recv, hop_send, load_sem, state_sem, out_sem, send_a, recv_a, send_f, recv_f,
):
    height, blocks, _, channels = raw.shape
    width = blocks * COLS
    layers = w_in.shape[0]
    units = expand.shape[2]
    tiles = width // Q_LON
    per = Q_LON // COLS
    bands = height // Q_LAT
    half = forward.shape[0] // 2
    part = Q_LAT * Q_LON
    keys = K_LAT * K_LON

    lat, lon = lax.axis_index("lat"), lax.axis_index("lon")
    n_lat, n_lon = lax.axis_size("lat"), lax.axis_size("lon")
    east, west = lax.rem(lon + 1, n_lon), lax.rem(lon + n_lon - 1, n_lon)
    has = {-1: lat > 0, 1: lat < n_lat - 1}

    def peer(dy, dx):
        return {"lat": lat + dy, "lon": {-1: west, 0: lon, 1: east}[dx]}

    odd = lax.rem(lat, 2) == 1
    even = jnp.logical_not(odd)
    paired = n_lat % 2 == 0
    far = {-1: lat >= 2, 1: lat <= n_lat - 3}
    detours = {-1: even & has[-1], 1: odd & has[1]}
    relays = {-1: even & far[1], 1: odd & far[-1]}

    def given(dy, f):
        if dy == 0:
            f()
        else:
            pl.when(has[dy])(f)

    plan = [(w_in, w_in_hbm, True), (taps, taps_hbm, False), (basis, basis_hbm, True),
            (w_out, w_out_hbm, True), (forward, forward_hbm, False), (expand, expand_hbm, True),
            (inverse, inverse_hbm, False), (shrink, shrink_hbm, True)]

    def load(i, layer):
        dst, src, layered = plan[i]
        view = (src.at[layer], dst.at[layer]) if layered else (src, dst)
        return pltpu.make_async_copy(*view, load_sem.at[i, layer])

    def transfer(buf, reach, send, recv, slot, dy, dx, rows, cols):
        r0, rn = rows
        c0, cn = cols
        to_r = r0 - dy * height
        to_c = c0 - dx * blocks
        return pltpu.make_async_remote_copy(
            src_ref=buf.at[pl.ds(reach + r0, rn), pl.ds(1 + c0, cn)],
            dst_ref=buf.at[pl.ds(reach + to_r, rn), pl.ds(1 + to_c, cn)],
            send_sem=send.at[slot],
            recv_sem=recv.at[slot],
            device_id=peer(dy, dx),
            device_id_type=MESH,
        )

    def edge(dy, reach):
        return (0, reach) if dy < 0 else (height - reach, reach)

    def column(dx):
        return (0, 1) if dx < 0 else (blocks - 1, 1)

    def copy_a(layer, kind, dy, dx, t=0):
        buf, send, recv = ext_a.at[layer], send_a.at[layer], recv_a.at[layer]
        if kind == "ns":
            slot = (tiles if dy > 0 else 0) + t
            return transfer(buf, RADIUS, send, recv, slot, dy, 0, edge(dy, RADIUS), (per * t, per))
        if kind == "ew":
            slot = 2 * tiles + (dx > 0)
            return transfer(buf, RADIUS, send, recv, slot, 0, dx, (0, height), column(dx))
        slot = 2 * tiles + 2 + 2 * (dy > 0) + (dx > 0)
        return transfer(buf, RADIUS, send, recv, slot, dy, dx, edge(dy, RADIUS), column(dx))

    def copy_f(layer, kind, dy, dx, b=0):
        buf, send, recv = ext_f.at[layer], send_f.at[layer], recv_f.at[layer]
        if kind == "ns":
            return transfer(
                buf, CONV_RADIUS, send, recv, int(dy > 0), dy, 0, edge(dy, CONV_RADIUS), (0, blocks)
            )
        if kind == "ew":
            slot = 6 + (bands if dx > 0 else 0) + b
            return transfer(
                buf, CONV_RADIUS, send, recv, slot, 0, dx, (Q_LAT * b, Q_LAT), column(dx)
            )
        slot = 2 + 2 * (dy > 0) + (dx > 0)
        return transfer(buf, CONV_RADIUS, send, recv, slot, dy, dx, edge(dy, CONV_RADIUS), column(dx))

    detour = tiles - 1

    def hop_in(dy):
        r0, rn = edge(dy, RADIUS)
        return pltpu.make_async_remote_copy(
            src_ref=ext_a.at[0, pl.ds(RADIUS + r0, rn), pl.ds(1 + per * detour, per)],
            dst_ref=hop,
            send_sem=send_a.at[0, (tiles if dy > 0 else 0) + detour],
            recv_sem=hop_recv,
            device_id={"lat": lat + 2 * dy, "lon": lon},
            device_id_type=MESH,
        )

    def hop_out(dy):
        r0, rn = edge(dy, RADIUS)
        return pltpu.make_async_remote_copy(
            src_ref=hop,
            dst_ref=ext_a.at[0, pl.ds(RADIUS + r0 - dy * height, rn), pl.ds(1 + per * detour, per)],
            send_sem=hop_send,
            recv_sem=recv_a.at[0, (tiles if dy > 0 else 0) + detour],
            device_id={"lat": lat - dy, "lon": lon},
            device_id_type=MESH,
        )

    def start_first(dy, t):
        if t != detour or not paired:
            copy_a(0, "ns", dy, 0, t).start()
        else:
            pl.when(detours[dy])(lambda: hop_in(dy).start())
            pl.when(jnp.logical_not(detours[dy]))(lambda: copy_a(0, "ns", dy, 0, t).start())

    def start_a(layer, t):
        for dy in (-1, 1):
            if isinstance(layer, int):
                given(dy, lambda dy=dy: start_first(dy, t))
            else:
                given(dy, lambda dy=dy: copy_a(layer, "ns", dy, 0, t).start())
        for dx, tile in ((-1, 0), (1, tiles - 1)):
            @pl.when(t == tile)
            def _():
                copy_a(layer, "ew", 0, dx).start()
                for dy in (-1, 1):
                    given(dy, lambda dy=dy: copy_a(layer, "corner", dy, dx).start())

    def wait_recv_a(layer, what):
        if what == "ew":
            for dx in (-1, 1):
                copy_a(layer, "ew", 0, dx).wait_recv()
        else:
            for dy in (-1, 1):
                def _():
                    for t in range(tiles):
                        copy_a(layer, "ns", dy, 0, t).wait_recv()
                    for dx in (-1, 1):
                        copy_a(layer, "corner", dy, dx).wait_recv()
                given(-dy, _)

    def wait_send_a(layer):
        for dx in (-1, 1):
            copy_a(layer, "ew", 0, dx).wait_send()
        for dy in (-1, 1):
            def _():
                for t in range(tiles):
                    copy_a(layer, "ns", dy, 0, t).wait_send()
                for dx in (-1, 1):
                    copy_a(layer, "corner", dy, dx).wait_send()
            given(dy, _)

    def start_f(layer, b):
        for dx in (-1, 1):
            copy_f(layer, "ew", 0, dx, b).start()

    def start_f_edge(layer, dy):
        def _():
            copy_f(layer, "ns", dy, 0).start()
            for dx in (-1, 1):
                copy_f(layer, "corner", dy, dx).start()
        given(dy, _)

    def wait_send_f(layer):
        for dx in (-1, 1):
            for b in range(bands):
                copy_f(layer, "ew", 0, dx, b).wait_send()
        for dy in (-1, 1):
            def _():
                copy_f(layer, "ns", dy, 0).wait_send()
                for dx in (-1, 1):
                    copy_f(layer, "corner", dy, dx).wait_send()
            given(dy, _)

    barrier = pltpu.get_barrier_semaphore()
    for dy in (-1, 0, 1):
        for dx in (-1, 0, 1):
            if (dy, dx) != (0, 0):
                given(dy, lambda dy=dy, dx=dx: pl.semaphore_signal(
                    barrier, inc=1, device_id=peer(dy, dx), device_id_type=MESH))
    if paired:
        for dy in (-1, 1):
            @pl.when(far[dy])
            def _():
                pl.semaphore_signal(
                    barrier, inc=1, device_id={"lat": lat + 2 * dy, "lon": lon}, device_id_type=MESH
                )

    state_copy = pltpu.make_async_copy(state_hbm, raw, state_sem)
    state_copy.start()

    def norm_tile(layer, t, x):
        z = norm_rows(x, gain_a_ref[pl.ds(layer, 1)]).reshape(height, per, COLS, channels)
        ext_a[layer, pl.ds(RADIUS, height), pl.ds(1 + per * t, per)] = z

    state_copy.wait()
    load(0, 0).start()

    @pl.loop(0, tiles)
    def _(t):
        x = raw[:, pl.ds(per * t, per)].astype(F32)
        stream[:, pl.ds(per * t, per)] = x
        norm_tile(0, t, x.reshape(height * Q_LON, channels))

    peers = 2 + 3 * sum(h.astype(jnp.int32) for h in has.values())
    if paired:
        peers = peers + sum(h.astype(jnp.int32) for h in far.values())
    pl.semaphore_wait(barrier, peers)

    for t in reversed(range(tiles)):
        start_a(0, t)

    load(1, 0).start()
    for layer in range(layers):
        load(2, layer).start()
    for i in range(3, len(plan)):
        load(i, 0).start()

    for dy in (-1, 1):
        @pl.when(jnp.logical_not(has[dy]))
        def _():
            for buf, reach in ((ext_a, RADIUS), (ext_f, CONV_RADIUS)):
                first = 0 if dy < 0 else reach + height
                shape = (layers, reach) + buf.shape[2:]
                buf[:, first : first + reach] = jnp.zeros(shape, BF16)

    m = lax.broadcasted_iota(jnp.int32, (part, keys), 0)
    n = lax.broadcasted_iota(jnp.int32, (part, keys), 1)
    up = n // K_LON - RADIUS - m // Q_LON
    over = n % K_LON - COLS - m % Q_LON
    near = (jnp.abs(up) <= RADIUS) & (jnp.abs(over) <= RADIUS)

    @pl.loop(0, bands)
    def _(b):
        place = lat * height + b * Q_LAT + n // K_LON - RADIUS
        bias_ref[b] = jnp.where(near & (place >= 0) & (place < n_lat * height), 0.0, NEG)

    def spectra():
        load(1, 0).wait()
        for layer in range(layers):
            load(2, layer).wait()

        @pl.loop(0, units // CHUNK)
        def _(c):
            lanes = pl.ds(pl.multiple_of(c * CHUNK, CHUNK), CHUNK)
            x = taps[:, :, :, lanes].astype(F32).reshape(-1, CHUNK)
            fill = jnp.zeros((basis.shape[2] // 2 - x.shape[0], CHUNK), F32)
            x = jnp.concatenate([x, fill], axis=0).astype(BF16)
            x = jnp.concatenate([x, x], axis=0)
            for layer in range(layers):
                khat[layer, :, lanes] = dot(basis[layer], x).astype(BF16)

        for layer in range(1, layers):
            for i, (_, _, layered) in enumerate(plan):
                if layered and i != 2:
                    load(i, layer).start()

    lane_head = lax.broadcasted_iota(jnp.int32, (part, SPAN), 1) // HEAD_DIM

    def attend(i, b, t, g):
        lo = g * SPAN
        rows, cols = pl.ds(b * Q_LAT, K_LAT), slice(per * t, per * t + K_LON // COLS)
        mine = slice(per * t, per * t + per)
        q = q_ref[pl.ds(b * Q_LAT, Q_LAT), mine, :, lo : lo + SPAN].reshape(part, SPAN)
        k = kv_ref[rows, cols, :, lo : lo + SPAN].reshape(keys, SPAN)
        v = kv_ref[rows, cols, :, channels + lo : channels + lo + SPAN].reshape(keys, SPAN)
        qq = jnp.concatenate(
            [jnp.where(lane_head == h, q, jnp.zeros_like(q)) for h in range(GROUP)], axis=0
        )
        s = lax.dot_general(qq, k, (((1,), (1,)), ((), ())), preferred_element_type=F32)
        s = (s.reshape(GROUP, part, keys) + bias_ref[b][None]).reshape(s.shape)
        return functools.partial(weigh, s, v, i, mine, lo)

    def weigh(s, v, i, mine, lo):
        e = jnp.exp(s - jnp.max(s, axis=-1, keepdims=True))
        total = jnp.sum(e, axis=-1, keepdims=True)
        o = dot(e.astype(BF16), v) * (1.0 / total)
        m = jnp.zeros((part, SPAN), F32)
        for h in range(GROUP):
            m = jnp.where(lane_head == h, o[h * part : (h + 1) * part], m)
        mixed_ref[i, :, mine, :, lo : lo + SPAN] = m.astype(BF16).reshape(Q_LAT, per, COLS, SPAN)

    def attend_all(i, b, ts):
        held = None
        for t in ts:
            for g in range(channels // SPAN):
                step = attend(i, b, t, g)
                if held is not None:
                    held()
                held = step
        held()

    own = slice(1, 1 + blocks)
    pairs = bands // 2

    def project(layer, rows, cols, count):
        x = ext_a[layer, rows, cols].reshape(-1, channels)
        y = dot(x, w_in[layer, :, channels:]).astype(BF16)
        kv_ref[rows, cols] = y.reshape(y.shape[0] // (count * COLS), count, COLS, 2 * channels)

    @pl.loop(0, layers)
    def _(layer):
        load(0, layer).wait()
        x = ext_a[layer, RADIUS : RADIUS + height, own].reshape(height * width, channels)
        shape = (height, blocks, COLS, channels)
        y = dot(x, w_in[layer, :, :channels]).astype(BF16) * (1.0 / math.sqrt(HEAD_DIM))
        q_ref[...] = y.astype(BF16).reshape(shape)
        y = dot(x, w_in[layer, :, channels:]).astype(BF16)
        kv_ref[RADIUS : RADIUS + height, own] = y.reshape(height, blocks, COLS, 2 * channels)

        @pl.when(layer == 0)
        def _():
            if paired:
                for dy in (-1, 1):
                    @pl.when(relays[dy])
                    def _():
                        hop_in(dy).wait_recv()
                        hop_out(dy).start()
            spectra()

        @pl.loop(0, pairs)
        def _(p):
            b0 = lax.rem(p + pairs - 1, pairs)
            both = (b0, bands - 1 - b0)

            @pl.when(b0 == 0)
            def _():
                wait_recv_a(layer, "rest")
                for r in (0, RADIUS + height):
                    project(layer, slice(r, r + RADIUS), slice(0, blocks + 2), blocks + 2)

            for i, b in enumerate(both):
                attend_all(i, b, range(1, tiles - 1))

                if i == 0:
                    @pl.when(p == 0)
                    def _():
                        wait_recv_a(layer, "ew")
                        for c in (0, 1 + blocks):
                            project(layer, slice(RADIUS, RADIUS + height), slice(c, c + 1), 1)
                        load(3, layer).wait()

                attend_all(i, b, (0, tiles - 1))
                rs = pl.ds(b * Q_LAT, Q_LAT)
                shape = (Q_LAT, blocks, COLS, channels)
                y = dot(mixed_ref[i].reshape(Q_LAT * width, channels), w_out[layer])
                y = y + stream[rs].reshape(Q_LAT * width, channels)
                stream[rs] = y.reshape(shape)
                z = norm_rows(y, gain_f_ref[pl.ds(layer, 1)])
                ext_f[layer, pl.ds(CONV_RADIUS + b * Q_LAT, Q_LAT), own] = z.reshape(shape)

                @pl.when(b0 == 0)
                def _():
                    start_f_edge(layer, 2 * i - 1)

                start_f(layer, b)

        @pl.when(layer == 0)
        def _():
            load(4, 0).wait()
            load(6, 0).wait()
        load(5, layer).wait()
        load(7, layer).wait()
        for dy in (-1, 1):
            given(-dy, lambda: copy_f(layer, "ns", dy, 0).wait_recv())

        @pl.loop(0, tiles)
        def _(k):
            t = lax.rem(k + 1, tiles)
            for dx, tile in ((-1, tiles - 1), (1, 0)):
                @pl.when(t == tile)
                def _():
                    for b in range(bands):
                        copy_f(layer, "ew", 0, dx, b).wait_recv()
                    for dy in (-1, 1):
                        given(-dy, lambda: copy_f(layer, "corner", dy, dx).wait_recv())
            x = ext_f[layer, :, pl.ds(per * t, per + 2)].reshape(-1, channels)
            nhat[...] = dot(forward[...], x).astype(BF16)

            @pl.loop(0, units // CHUNK)
            def _(c):
                lanes = pl.ds(pl.multiple_of(c * CHUNK, CHUNK), CHUNK)
                z = dot(nhat[...], expand[layer, :, lanes]).astype(BF16)
                re, im = z[:half], z[half:]
                k_re, k_im = khat[layer, :half, lanes], khat[layer, half:, lanes]
                y = jnp.concatenate([re * k_re - im * k_im, re * k_im + im * k_re], axis=0)
                act[:, lanes] = gelu(dot(inverse[...], y)).astype(BF16)

            cs = pl.ds(per * t, per)
            y = dot(act[...], shrink[layer]) + stream[:, cs].reshape(height * Q_LON, channels)
            shape = (height, per, COLS, channels)

            @pl.when(layer < layers - 1)
            def _():
                stream[:, cs] = y.reshape(shape)
                norm_tile(layer + 1, t, y)
                start_a(layer + 1, t)

            @pl.when(layer == layers - 1)
            def _():
                raw[:, cs] = y.astype(BF16).reshape(shape)
                pltpu.make_async_copy(raw.at[:, cs], out_hbm.at[:, cs], out_sem.at[t]).start()

    for t in range(tiles):
        cs = pl.ds(per * t, per)
        pltpu.make_async_copy(raw.at[:, cs], out_hbm.at[:, cs], out_sem.at[t]).wait()
    if paired:
        for dy in (-1, 1):
            pl.when(relays[dy])(lambda: hop_out(dy).wait_send())
    for layer in range(layers):
        wait_send_a(layer)
        wait_send_f(layer)


def per_device(
    state,
    attention_in,
    attention_out,
    expand_weight,
    depth_kernel,
    shrink_weight,
    norm_attention,
    norm_feedforward,
):
    height, width, channels = state.shape
    layers, side, _, units = depth_kernel.shape
    blocks = width // COLS
    tiles, bands = width // Q_LON, height // Q_LAT
    forward, basis, inverse = spectral(height, Q_LON, layers)
    taps = depth_kernel.transpose(1, 2, 0, 3)
    heavy = (
        attention_in, attention_out, expand_weight, shrink_weight, taps,
        jnp.asarray(forward), jnp.asarray(basis), jnp.asarray(inverse),
    )
    any_spec = pl.BlockSpec(memory_space=pl.ANY)
    vmem_spec = pl.BlockSpec(memory_space=pltpu.VMEM)
    shape = (height, blocks, COLS, channels)
    slots_a, slots_f = 2 * tiles + 6, 2 * bands + 6
    out = pl.pallas_call(
        kernel,
        out_shape=jax.ShapeDtypeStruct(shape, BF16),
        in_specs=[any_spec] + [vmem_spec] * 2 + [any_spec] * len(heavy),
        out_specs=any_spec,
        scratch_shapes=[pltpu.VMEM(a.shape, BF16) for a in heavy]
        + [
            pltpu.VMEM(shape, BF16),
            pltpu.VMEM((layers, height + 2 * RADIUS, blocks + 2, COLS, channels), BF16),
            pltpu.VMEM((layers, height + 2 * CONV_RADIUS, blocks + 2, COLS, channels), BF16),
            pltpu.VMEM(shape, F32),
            pltpu.VMEM(shape, BF16),
            pltpu.VMEM((height + 2 * RADIUS, blocks + 2, COLS, 2 * channels), BF16),
            pltpu.VMEM((2, Q_LAT, blocks, COLS, channels), BF16),
            pltpu.VMEM((bands, Q_LAT * Q_LON, K_LAT * K_LON), F32),
            pltpu.VMEM((forward.shape[0], channels), BF16),
            pltpu.VMEM((layers, forward.shape[0], units), BF16),
            pltpu.VMEM((height * Q_LON, units), BF16),
            pltpu.VMEM((RADIUS, Q_LON // COLS, COLS, channels), BF16),
            pltpu.SemaphoreType.DMA,
            pltpu.SemaphoreType.DMA,
            pltpu.SemaphoreType.DMA((len(heavy), layers)),
            pltpu.SemaphoreType.DMA,
            pltpu.SemaphoreType.DMA((tiles,)),
            pltpu.SemaphoreType.DMA((layers, slots_a)),
            pltpu.SemaphoreType.DMA((layers, slots_a)),
            pltpu.SemaphoreType.DMA((layers, slots_f)),
            pltpu.SemaphoreType.DMA((layers, slots_f)),
        ],
        compiler_params=pltpu.CompilerParams(
            vmem_limit_bytes=VMEM_LIMIT, collective_id=0, has_side_effects=True
        ),
        name="blocks",
    )(
        state.reshape(shape), norm_attention, norm_feedforward, *heavy
    )
    return out.reshape(height, width, channels)


def solution(mesh):
    in_specs = (P("lat", "lon", None), P(), P(), P(), P(), P(), P(), P())
    out_specs = P("lat", "lon", None)
    return jax.shard_map(
        per_device, mesh=mesh, in_specs=in_specs, out_specs=out_specs, check_vma=False
    )
```
